32 devices in a mesh: grp: 2 (over x), ep: 8 (over z, y), dp: 2 (over core).
Axes of the slice: x: 2, y: 2, z: 4, core: 2. Of those that a mesh axis runs over, the one named last changes fastest.
Arguments:
- tokens: bfloat16 [2, 1024, 2048], P(None, ('grp', 'ep', 'dp')), parts along dimension 1, may hold values from -6 to 6
- norm_gain: float32 [2048], replicated, may hold values from 0.25 to 1.75
- expert_ids: int32 [2, 1024, 8], P(None, ('grp', 'ep', 'dp')), parts along dimension 1, may hold values from 0 to 15, all different within a row; in each aligned block of 32 rows (0 to 31, 32 to 63, ..., all dimensions but the last counted through in order) at most 24 rows name the same one
- gate_probs: float32 [2, 1024, 8], P(None, ('grp', 'ep', 'dp')), parts along dimension 1, may hold values from 0.05 to 1
- expert_weights: bfloat16 [16, 3, 2048, 768], P(('ep', 'dp')), may hold values from -0.125 to 0.125
Outputs:
- combined: bfloat16 [2, 1024, 2048], P(None, ('grp', 'ep', 'dp')), parts along dimension 1
The draws below stay inside these ranges and needn't reach their ends.
There are 2 independent parts, one for each index of `grp`. The reference program is written for one: setup_inputs(seed, part) draws one part's arguments, and reference() takes and returns one part's arrays. A program takes and returns all parts, laid end to end along the dimension named above; an argument that names none is the same for every part. Nothing has to cross between parts.
Inputs may be any that keep to these rules, and one draw needn't show every extreme that they name: `expert_ids`: each token names 8 different experts. In each step the 32 tokens of one device (aligned blocks of 32 rows) name any one expert at most 24 times, a bound that some block reaches; every expert is named somewhere.
All inputs are finite; a program needn't handle non-finite values.
Results may differ from the reference program's by a relative error of at most 0.0072.
Values may be sent and summed in bfloat16 or wider, within the bound.
A program may use at most 128 MiB of HBM per device.

```python
import math
import jax
import jax.numpy as jnp
import numpy as np
from jax import lax

D = 2048
FF = 768
TOP = 8
STEPS = 2
TOK_DEV = 32
EXPERTS = 16
TOKENS = 512
CAP = 24


def levels(rng, shape, shards, low, high):
    def one(dim, parts):
        heights = jax.random.uniform(jax.random.fold_in(jax.random.fold_in(rng, 6), dim), (parts,), jnp.float32, low / len(shards), high / len(shards))
        return jnp.repeat(jnp.exp(heights), shape[dim] // parts).reshape((-1,) + (1,) * (len(shape) - dim - 1))

    level = one(*shards[0])
    for cut in shards[1:]:
        level = level * one(*cut)
    return level


def assign_block(key, own, number, rows, count, top, most, lean):
    sequence = jax.random.permutation(key, count)
    crowded, usual = shares(count, rows * top, most, lean, True), shares(count, rows * top, most, lean, False)
    places = jnp.arange(count)

    def named(lengths, turn):
        used = int((lengths > 0).sum())
        fixed = max(1, used // 4)
        shifted = fixed + (places - fixed + turn * (used - fixed)) % max(1, count - fixed)
        return jnp.zeros((count,), jnp.int32).at[sequence[jnp.where(places < fixed, places, shifted)]].set(jnp.asarray(lengths, jnp.int32))

    lengths = jnp.where(number % 4 == 0, named(crowded, number // 4), named(usual, number - number // 4 - 1))
    mixed = jax.random.permutation(jax.random.fold_in(own, 3), count)
    giver, taker = mixed[0:count // 2 * 2:2], mixed[1:count // 2 * 2:2]
    room = jnp.minimum(lengths[giver] - 1, most - lengths[taker]) // 2
    room = jnp.where((giver == sequence[0]) | (taker == sequence[0]) | (lengths[taker] == 0), 0, jnp.maximum(room, 0))
    shifted = jax.random.randint(jax.random.fold_in(own, 4), (count // 2,), 0, 1 << 20) % (room + 1)
    lengths = lengths.at[giver].add(-shifted).at[taker].add(shifted)
    members = jnp.searchsorted(jnp.cumsum(lengths), jnp.arange(rows * top), side="right").astype(jnp.int32)
    table = members.reshape(top, rows).T
    table = table[jax.random.permutation(jax.random.fold_in(own, 1), rows)]
    turn = jax.random.randint(jax.random.fold_in(own, 2), (rows, 1), 0, top)
    return jnp.take_along_axis(table, (jnp.arange(top)[None, :] + turn) % top, axis=1)


def shares(count, total, limit, slope, full):
    weights = [(1 << 20) // math.isqrt(rank ** slope) + 1 for rank in range(1, count + 1)]
    largest = limit if full else min(limit, max(-(-total // count), total * weights[0] // sum(weights)))
    least = 1 if total - largest >= count - 1 else 0
    holding, surplus = [largest] + [least] * (count - 1), total - largest - least * (count - 1)
    while surplus > 0:
        candidates = [i for i in range(1, count) if holding[i] < largest] or [i for i in range(1, count) if holding[i] < limit]
        pool, budget = sum([weights[i] for i in candidates]), surplus
        for i in candidates:
            addition = min(limit - holding[i], max(1, budget * weights[i] // pool), surplus)
            holding[i] = holding[i] + addition
            surplus = surplus - addition
    return np.array(holding)


def scatter_about(rng, shape, scale, bound, pieces=(), held_as=jnp.bfloat16):
    values = scale * jax.random.normal(rng, shape, jnp.float32)
    if pieces:
        values = values * levels(rng, shape, pieces, -0.22, 0.18)
    return jnp.clip(values, -bound, bound).astype(held_as)


def setup_inputs(seed: int = 0, part: int = 0) -> dict:
    streams_of = jax.random.split(jax.random.key(seed), 6)
    part_splits = jax.random.split(jax.random.fold_in(streams_of[5], part), 6)
    tokens = scatter_about(part_splits[0], (STEPS, TOKENS, D), 1.0, 6.0, ((1, 16),))
    norm_gain = jnp.clip(1.0 + 0.15 * jax.random.normal(streams_of[1], (D,), jnp.float32), 0.25, 1.75)
    expert_ids_keys = jax.random.split(jax.random.fold_in(part_splits[2], 1), STEPS * TOKENS // TOK_DEV)
    expert_ids_turns = jax.random.permutation(jax.random.fold_in(part_splits[2], 3), STEPS * TOKENS // TOK_DEV)
    expert_ids = jax.vmap(lambda own, number: assign_block(jax.random.fold_in(part_splits[2], 2), own, number, TOK_DEV, EXPERTS, TOP, CAP, 2))(expert_ids_keys, expert_ids_turns).reshape((STEPS, TOKENS, TOP))
    gate_probs = jnp.clip(jnp.exp(math.log(1.0) - 2.9957323 * jax.random.uniform(part_splits[3], (STEPS, TOKENS, TOP), jnp.float32) ** levels(part_splits[3], (STEPS, TOKENS, TOP), ((1, 16),), -0.2, 0.2)), 0.05, 1.0)
    expert_weights = scatter_about(streams_of[4], (EXPERTS, 3, D, FF), D ** -0.5, 0.125, ((0, 16),))
    return dict(tokens=tokens, norm_gain=norm_gain, expert_ids=expert_ids, gate_probs=gate_probs, expert_weights=expert_weights)


def norm_rows(hidden_rows, norm_gain):
    values = hidden_rows.astype(jnp.float32)
    inverse_rms = lax.rsqrt(lax.optimization_barrier(jnp.mean(values * values, axis=-1, keepdims=True)) + 1e-06)
    return (values * inverse_rms * norm_gain).astype(jnp.bfloat16)

def expert_rows(row_block, weights):
    gate_part = jnp.dot(row_block, weights[0], preferred_element_type=jnp.float32)
    up_part = jnp.dot(row_block, weights[1], preferred_element_type=jnp.float32)
    hidden = (jax.nn.silu(gate_part) * up_part).astype(jnp.bfloat16)
    return lax.dot_general(hidden, weights[2], (((1,), (1,)), ((), ())), preferred_element_type=jnp.float32)

def one_step(step_tokens, norm_gain, step_ids, step_probs, expert_weights):
    normed = norm_rows(step_tokens, norm_gain)
    share = step_probs / lax.optimization_barrier(jnp.sum(step_probs, axis=1, keepdims=True))
    flat_ids = step_ids.reshape(-1).astype(jnp.int32)
    flat_share = share.reshape(-1)
    row_limit = EXPERTS * CAP

    def per_expert(running, expert):
        chosen = (flat_ids == expert).astype(jnp.int32)
        picked = jnp.argsort(1 - chosen, stable=True)[:row_limit].astype(jnp.int32)
        valid = jnp.arange(row_limit, dtype=jnp.int32) < jnp.sum(chosen)
        token_index = (picked // TOP).astype(jnp.int32)
        picked_rows = normed[token_index]
        produced = expert_rows(picked_rows, expert_weights[expert]).astype(jnp.bfloat16)
        weighted = jnp.where(valid[:, None], flat_share[picked][:, None] * produced.astype(jnp.float32), jnp.zeros((), jnp.float32))
        return (running.at[token_index].add(weighted), None)
    start_sum = jnp.zeros(normed.shape, jnp.float32)
    total_sum, _ = lax.scan(per_expert, start_sum, jnp.arange(EXPERTS, dtype=jnp.int32))
    return total_sum.astype(jnp.bfloat16)

def reference(tokens, norm_gain, expert_ids, gate_probs, expert_weights):
    results = []
    for decode_step in range(STEPS):
        results.append(one_step(tokens[decode_step], norm_gain, expert_ids[decode_step], gate_probs[decode_step], expert_weights))
    return jnp.stack(results)
```

```python
import functools

import jax
import jax.numpy as jnp
from jax import lax
from jax.experimental import pallas as pl
from jax.experimental.pallas import tpu as pltpu
from jax.sharding import PartitionSpec as P

NZ = 4
NY = 2
LANES = 128
PIECES = 1
F_TILE = 256
LEAPS = 0
DIRECT = 1
ROW = 6
PLANS = (
    (
        1520640, -1340066800, -2147377024, 33620225, -1601142782, 17891345,
        -1337982447, -1600126958, 2163716, 35717409, -1605369822, 68460736,
        21037121, -1335885247, 606273602, 872947875, 5349584, 608371025,
        38871235, -1334837166, 6398176, 39911777, 6423636, 7446768,
        -1607466639, 73663089, -1599078286, 676528177, 36766001, 3277940,
        873990243, 545796136, 67707032, 810026036, 68755624, 542640243,
        405348552, 407449704, 813179096, 553132264, 540551219, 548932697,
        208232454, 209281046, 986169, 983055, 983055, 983055,
    ),
    (
        1520640, -1340066800, -2147376000, -1534066431, -1337982463, 1146882,
        17932448, -1336933871, 1220800, 2163732, 35717409, 2269280,
        69509328, 21037121, 37855344, 71565378, 874001416, -1595932591,
        673382737, -1594883503, 675479634, 72658992, 23134305, 6423137,
        807968944, 14877795, 24182897, 676528753, 74711154, 19988529,
        3277361, 70518899, 613950600, 547893320, 811074585, 543695048,
        544743640, 552078377, 553126985, 1686448179, 409546808, 207167672,
        209281030, 205086742, 984073, 983055, 983055, 983055,
    ),
    (
        3619872, -1275055056, -1203724128, 18972705, -2145254879, -1273977680,
        3254352, 36766001, -1602176928, 65586, -1598029567, 33663184,
        70516738, -1200619455, 21078160, 4325953, 67412192, 23134305,
        6423137, 137404656, 608372912, 1122499, 17901571, 73662993,
        5308434, 38863185, 5374996, 24182897, 72614513, 7525541,
        876100648, 872949779, 547882100, 616052808, 676869144, 545798248,
        70854739, 685252808, 946026616, 552083608, -802809783, 553126921,
        146278456, 69810291, -801764327, 208211033, 986233, 983055,
    ),
    (
        3619872, -1543490512, -1203724128, 18972705, -1542414160, 35764304,
        -2145213312, -1597986720, 69510288, 19988529, -1469054415, 3317968,
        66612, 33620225, 174304, 137406704, 545465347, 21037121,
        4325953, 6358084, 39911777, 1114210, 17901635, 1180177,
        22085713, 38863892, 7405650, 72614257, 40973411, 820183154,
        -802805741, 1009255540, 604517432, 676536488, 548943944, 945300504,
        612893737, 549988456, 70853784, 947071096, 403251416, 687352040,
        206112824, 409587766, 207162393, 986233, 983055, 983055,
    ),
    (
        5717056, -1201653680, -1272930112, 21069889, -2143157695, -1200576304,
        5350448, 38863185, -1595886592, 6357074, -1600126623, 39953584,
        72613986, -1274019807, 18981104, 2228769, 73703552, 16842753,
        131585, 72392848, 606274768, 7413923, 24193123, 67371633,
        3211378, 36766001, 70516786, 17891345, 74711569, 1225925,
        945306696, 549992552, 674444328, 685245460, 607664248, 552088584,
        547882073, 678634680, 553137176, 545798147, 208214057, 72884376,
        -1337588520, 940770377, -1336538055, 201919609, 986137, 983055,
    ),
    (
        5717056, -1470089136, -1272930112, 21069889, -1469013808, 37860400,
        -2143115040, -1600084992, 71608560, 22085713, -1542454703, 5415088,
        6358100, 39911777, 6464640, 72393872, 551756899, 18939937,
        2228769, 66596, 33620225, 3211266, 19998755, 3277361,
        24182897, 7471729, 1115252, 70517009, 34681859, 813891602,
        1011396678, 678626324, 677918808, 875045064, 678961368, 71906360,
        674441448, 547890184, 72952056, 548938776, 612898921, 940778648,
        204014680, -1336535031, 205065337, 986137, 983055, 983055,
    ),
    (
        7813216, -1337968528, -2141085472, 39911777, -1594851230, 24182897,
        -1340079503, -1598029710, 4260964, 37814593, -1607466942, 74752160,
        18939937, -1342176735, 608370722, 946348227, 3252400, 606273841,
        36774051, -1341128654, 106624, 33620225, 132148, 1155216,
        -1605369583, 67371537, -1596981230, 674431057, 38863185, 5374996,
        947390467, 552087624, 73998584, 807928916, 75047112, 540542995,
        407445672, 405352456, 806887608, 546840712, 542648403, 551029817,
        201941094, 1618349081, 986201, 983055, 983055, 983055,
    ),
    (
        7813216, -1337968528, -2141083424, -1460666015, -1340079519, 7438434,
        24223936, -1339030927, 7512224, 4260980, 37814593, 4366336,
        71606448, 18939937, 35758096, 69468194, 947402856, -1602224079,
        675479857, -1601174991, 673382450, 70561872, 16842753, 131585,
        810066128, 8586243, 17891345, 674431505, 68419602, 22085713,
        5374545, 72615955, 687352040, 549990440, 808977529, 537403560,
        538452152, 1692732489, 676536456, 546835497, 403255384, 205070552,
        1618370662, 73993241, 986201, 983055, 983055, 983055,
    ),
)


def norm_rows(hidden_rows, norm_gain):
    values = hidden_rows.astype(jnp.float32)
    inverse_rms = lax.rsqrt(jnp.mean(values * values, axis=-1, keepdims=True) + 1e-06)
    return (values * inverse_rms * norm_gain).astype(jnp.bfloat16)


def expert_rows(row_block, weights):
    gate_part = jnp.dot(row_block, weights[0], preferred_element_type=jnp.float32)
    up_part = jnp.dot(row_block, weights[1], preferred_element_type=jnp.float32)
    hidden = (jax.nn.silu(gate_part) * up_part).astype(jnp.bfloat16)
    return lax.dot_general(
        hidden, weights[2], (((1,), (1,)), ((), ())), preferred_element_type=jnp.float32
    )


def gather_scatter_form(tokens, norm_gain, expert_ids, gate_probs, expert_weights):
    axes = ("ep", "dp")
    experts = lax.axis_size("ep") * lax.axis_size("dp")
    me = lax.axis_index(axes)
    steps_total, tok_count, width = tokens.shape
    rows = steps_total * tok_count
    normed = norm_rows(tokens.reshape(rows, width), norm_gain)
    share = gate_probs / jnp.sum(gate_probs, axis=-1, keepdims=True)
    hits = expert_ids[..., None] == lax.broadcasted_iota(jnp.int32, (1, 1, 1, experts), 3)
    dense_share = jnp.sum(jnp.where(hits, share[..., None], 0.0), axis=2).reshape(rows, experts)
    all_rows = lax.all_gather(normed, axes, tiled=True)
    all_share = lax.all_gather(dense_share, axes, tiled=True)
    mine = lax.broadcasted_iota(jnp.int32, (1, experts), 1) == me
    row_share = jnp.sum(jnp.where(mine, all_share, 0.0), axis=1, keepdims=True)
    expert_out = expert_rows(all_rows, expert_weights[0])
    weighted = (row_share * expert_out).astype(jnp.bfloat16)
    combined = lax.psum_scatter(weighted, axes, scatter_dimension=0, tiled=True)
    return combined.reshape(steps_total, tok_count, width)


def moe_kernel(
    tok_hbm, gain_hbm, ids_hbm, prob_hbm, w_hbm, out_ref,
    tok, gain, ids, prob, x, wv, hid, scale, ob, sr, ys, yr, zs, zr,
    in_sem, w_sem, x_recv, x_send, c_recv, c_send, y_recv, y_send, z_recv, z_send,
):
    steps, toks, width = tok.shape
    top = ids.shape[1]
    ff = wv.shape[2]
    cols = width // PIECES
    experts = lax.axis_size("ep") * lax.axis_size("dp")
    ep = lax.axis_index("ep")
    c = lax.axis_index("dp")
    z = ep // NY
    y = ep % NY
    me = ep * 2 + c

    sib = {"ep": ep, "dp": 1 - c}
    ynb = {"ep": z * NY + 1 - y, "dp": c}
    zup = {"ep": (z + 1) % NZ * NY + y, "dp": c}
    zdn = {"ep": (z + NZ - 1) % NZ * NY + y, "dp": c}
    zfar = {"ep": (NZ - 1 - z) * NY + y, "dp": c}
    can_up = z < NZ - 1
    can_dn = z > 0
    outer = (z == 0) | (z == NZ - 1)

    barrier = pltpu.get_barrier_semaphore()
    for peer in (sib, ynb):
        pl.semaphore_signal(barrier, inc=1, device_id=peer)

    @pl.when(can_up)
    def _():
        pl.semaphore_signal(barrier, inc=1, device_id=zup)

    @pl.when(can_dn)
    def _():
        pl.semaphore_signal(barrier, inc=1, device_id=zdn)

    if LEAPS:
        @pl.when(outer)
        def _():
            pl.semaphore_signal(barrier, inc=1, device_id=zfar)

    loads = [
        pltpu.make_async_copy(tok_hbm, tok, in_sem.at[0]),
        pltpu.make_async_copy(gain_hbm, gain, in_sem.at[1]),
        pltpu.make_async_copy(ids_hbm, ids, in_sem.at[2]),
        pltpu.make_async_copy(prob_hbm, prob, in_sem.at[3]),
    ]
    for load in loads:
        load.start()
    for i in range(3):
        pltpu.make_async_copy(w_hbm.at[0, i], wv.at[i], w_sem.at[i]).start()

    def choose(values, index):
        value = jnp.int32(values[0])
        for place in range(1, len(values)):
            value = jnp.where(index == place, jnp.int32(values[place]), value)
        return value

    words = [choose(column, 2 * z + c) for column in zip(*PLANS)]

    for load in loads:
        load.wait()

    def norm(s):
        x[s, z, c, y, :, :width] = norm_rows(tok[s], gain[...])

    def shares(s):
        probs = prob[s]
        share = probs / jnp.sum(probs, axis=0, keepdims=True)
        named = ids[s]
        row = lax.broadcasted_iota(jnp.int32, (2 * experts, toks), 0)
        both = jnp.zeros((2 * experts, toks), jnp.float32)
        for i in range(top):
            hit = (row == named[i : i + 1]) | (row == named[i : i + 1] + experts)
            both = jnp.where(hit, share[i : i + 1], both)
        high = both.astype(jnp.bfloat16).astype(jnp.float32)
        pieces = jnp.where(row < experts, high, both - high).astype(jnp.bfloat16)
        eye = (
            lax.broadcasted_iota(jnp.int32, (2 * experts, LANES), 0) + 2 * experts * s
            == lax.broadcasted_iota(jnp.int32, (2 * experts, LANES), 1)
        ).astype(jnp.float32).astype(jnp.bfloat16)
        return lax.dot_general(
            pieces, eye, (((0,), (0,)), ((), ())), preferred_element_type=jnp.float32
        )

    norm(0)
    x[0, z, c, y, :, width:] = (shares(0) + shares(1)).astype(jnp.bfloat16)
    peers = 2 + jnp.where(can_up, 1, 0) + jnp.where(can_dn, 1, 0)
    if LEAPS:
        peers = peers + jnp.where(outer, 1, 0)
    pl.semaphore_wait(barrier, peers)

    def x_copy(s, k, col, row, far, act, do):
        peer = (zup, zdn, ynb, sib, zfar)[act]
        for block, here in (
            (x.at[s, k, col, row], s == 0),
            (x.at[s, k, col, row, :, :width], s > 0),
        ):
            @pl.when(here)
            def _(block=block):
                do(pltpu.make_async_remote_copy(
                    block, block, x_send.at[s, k, far, act], x_recv.at[s, k, col, row],
                    device_id=peer,
                ))

    def c_copy(n, p):
        return pltpu.make_async_remote_copy(
            ob.at[n, p, 1 - c], sr.at[n, p], c_send.at[n, p], c_recv.at[n, p], device_id=sib
        )

    def y_copy(n, p):
        return pltpu.make_async_remote_copy(
            ys.at[n, p], yr.at[n, p], y_send.at[n, p], y_recv.at[n, p], device_id=ynb
        )

    def z_copy(n, p, far, source, target):
        return pltpu.make_async_remote_copy(
            zs.at[n, p, far], zr.at[source, n, p, far], z_send.at[n, p, far],
            z_recv.at[source, n, p, far], device_id={"ep": target * NY + y, "dp": c},
        )

    def start(copy):
        copy.start()

    def sent(copy):
        copy.wait_send()

    def got(copy):
        copy.wait_recv()

    def f32(value):
        return value.astype(jnp.float32)

    def do_relay(s, k, far, p, bits):
        row = jnp.where(far == 1, 1 - y, y)

        @pl.when(bits >= 32)
        def _():
            x_copy(s, k, c, row, far, 2, got)

        for act in range(4 + LEAPS):
            @pl.when(bits // 2**act % 2 == 1)
            def _(act=act):
                x_copy(s, k, c, row, far, act, start)

    def do_sent(s, k, far, p, bits):
        row = jnp.where(far == 1, 1 - y, y)
        for act in range(4 + LEAPS):
            @pl.when(bits // 2**act % 2 == 1)
            def _(act=act):
                x_copy(s, k, c, row, far, act, sent)

    def do_norm(s, k, far, p, bits):
        norm(1)

    def do_hidden(s, k, far, p, bits):
        @pl.when(bits >= 32)
        def _():
            for i in range(2):
                pltpu.make_async_copy(w_hbm.at[0, i], wv.at[i], w_sem.at[i]).wait()

        @pl.when(p == 0)
        def _():
            for row in range(NY):
                x_copy(s, k, 1 - c, row, 0, 3, got)

            rows = 4 * toks
            lane = lax.broadcasted_iota(jnp.int32, (rows, LANES), 1) - 2 * experts * s
            parts = f32(x[0, k, :, :, :, width:].reshape(rows, LANES))
            mine = (lane == me) | (lane == me + experts)
            share = jnp.sum(jnp.where(mine, parts, 0.0), axis=1, keepdims=True)
            scale[...] = jnp.broadcast_to(share, (rows, LANES))

        block = x[s, k, :, :, :, :width].reshape(4 * toks, width)
        here = pl.ds(pl.multiple_of(p * F_TILE, F_TILE), F_TILE)
        gate = jnp.dot(block, wv[0, :, here], preferred_element_type=jnp.float32)
        up = jnp.dot(block, wv[1, :, here], preferred_element_type=jnp.float32)
        hid[:, here] = (gate / (1.0 + jnp.exp(-gate)) * up).astype(jnp.bfloat16)

    def do_out(s, k, far, p, bits):
        @pl.when(bits >= 32)
        def _():
            pltpu.make_async_copy(w_hbm.at[0, 2], wv.at[2], w_sem.at[2]).wait()

        n = s * NZ + k
        hidden = hid[...]
        tile = 256
        share = jnp.concatenate([scale[...]] * (tile // LANES), axis=1)
        for d in range(0, cols, tile):
            part = lax.dot_general(
                hidden, wv[2, pl.ds(pl.multiple_of(p * cols + d, tile), tile), :],
                (((1,), (1,)), ((), ())), preferred_element_type=jnp.float32,
            )
            ob[n, p, :, :, :, d : d + tile] = (
                (share * part).astype(jnp.bfloat16).reshape(2, NY, toks, tile)
            )
        c_copy(n, p).start()

    def pair(n, p, row):
        return f32(ob[n, p, c, row]) + f32(sr[n, p, row])

    def first_waits(n, p, bits):
        @pl.when(bits % 2 == 1)
        def _():
            c_copy(n, p).wait_recv()

        @pl.when(bits // 2 % 2 == 1)
        def _():
            y_copy(n, p).wait_recv()

    def do_cross(s, k, far, p, bits):
        n = s * NZ + k
        first_waits(n, p, bits)
        ys[n, p] = pair(n, p, 1 - y).astype(jnp.bfloat16)
        y_copy(n, p).start()

    def do_pass(s, k, far, p, bits):
        n = s * NZ + k
        row = jnp.where(far == 1, 1 - y, y)
        first_waits(n, p, bits)

        step = jnp.where(k > z, 1, -1)
        before = jnp.clip(z - step, 0, NZ - 1)

        @pl.when(bits // 4 % 2 == 1)
        def _():
            z_copy(n, p, far, before, z).wait_recv()

        @pl.when(bits // 2 % 4 == 3)
        def _():
            zs[n, p, far] = (
                pair(n, p, row) + f32(yr[n, p]) + f32(zr[before, n, p, far])
            ).astype(jnp.bfloat16)

        @pl.when(bits // 2 % 4 == 2)
        def _():
            zs[n, p, far] = (pair(n, p, row) + f32(zr[before, n, p, far])).astype(jnp.bfloat16)

        @pl.when(bits // 2 % 4 == 1)
        def _():
            zs[n, p, far] = (pair(n, p, row) + f32(yr[n, p])).astype(jnp.bfloat16)

        @pl.when(bits // 2 % 4 == 0)
        def _():
            zs[n, p, far] = pair(n, p, row).astype(jnp.bfloat16)

        @pl.when(bits // 8 % 2 == 0)
        def _():
            z_copy(n, p, far, z, z + step).start()

        if DIRECT:
            @pl.when(bits // 8 % 2 == 1)
            def _():
                z_copy(n, p, far, z, k).start()

    def arrived(n, p, far, row, bits):
        total = pair(n, p, row)
        for source in range(NZ):
            named = bits // (4 * 2**source) % 2 == 1

            @pl.when(named)
            def _(source=source):
                z_copy(n, p, far, source, (z + 1) % NZ).wait_recv()

            total = total + jnp.where(named, f32(zr[source, n, p, far]), 0.0)
        return total

    def do_hand(s, k, far, p, bits):
        n = s * NZ + k
        first_waits(n, p, bits % 2)
        ys[n, p] = arrived(n, p, 1, 1 - y, bits).astype(jnp.bfloat16)
        y_copy(n, p).start()

    def do_final(s, k, far, p, bits):
        n = s * NZ + k
        first_waits(n, p, bits % 2 + 2)
        total = arrived(n, p, 0, y, bits) + f32(yr[n, p])
        here = pl.ds(pl.multiple_of(p * cols, cols), cols)
        out_ref[s, :, here] = total.astype(jnp.bfloat16)

    def do_settle(s, k, far, p, bits):
        n = s * NZ + k
        c_copy(n, p).wait_send()

        @pl.when(bits % 2 == 1)
        def _():
            y_copy(n, p).wait_send()

        for lane in range(2):
            @pl.when(bits // (2 + 2 * lane) % 2 == 1)
            def _(lane=lane):
                z_copy(n, p, lane, z, (z + 1) % NZ).wait_send()

    kinds = (
        (do_relay, do_hidden, do_out),
        (do_pass, do_cross, do_hand, do_final),
        (do_norm, do_sent, do_settle),
    )

    def obey(code):
        kind = code % 16
        s = code // 16 % 2
        k = code // 32 % 4
        far = code // 128 % 2
        p = code // 256 % 4
        bits = code // 1024
        first = 0
        for some in kinds:
            @pl.when((kind >= first) & (kind < first + len(some)))
            def _(first=first, some=some):
                for number, body in enumerate(some):
                    @pl.when(kind == first + number)
                    def _(body=body):
                        body(s, k, far, p, bits)

            first += len(some)

    blocks = len(words) // ROW

    def block(b, carry):
        row = [choose(words[j::ROW], b) for j in range(ROW)]

        def entry(i, carry):
            word = choose(row, i // 2)
            obey(jnp.where(i % 2 == 0, word & 65535, (word >> 16) & 65535))
            return carry

        lax.fori_loop(0, 2 * ROW, entry, 0)
        return carry

    lax.fori_loop(0, blocks, block, 0)


def kernel_form(tokens, norm_gain, expert_ids, gate_probs, expert_weights):
    steps, toks, width = tokens.shape
    top = expert_ids.shape[2]
    ff = expert_weights.shape[3]
    groups = steps * NZ
    cols = width // PIECES
    half = jnp.bfloat16
    hbm = pl.BlockSpec(memory_space=pltpu.MemorySpace.HBM)
    dma = pltpu.SemaphoreType.DMA
    rows = groups * 4 * toks
    return pl.pallas_call(
        moe_kernel,
        out_shape=jax.ShapeDtypeStruct((steps, toks, width), half),
        in_specs=[hbm, hbm, hbm, hbm, hbm],
        out_specs=pl.BlockSpec(memory_space=pltpu.VMEM),
        scratch_shapes=[
            pltpu.VMEM((steps, toks, width), half),
            pltpu.VMEM((1, width), jnp.float32),
            pltpu.VMEM((steps, top, toks), jnp.int32),
            pltpu.VMEM((steps, top, toks), jnp.float32),
            pltpu.VMEM((steps, NZ, 2, NY, toks, width + LANES), half),
            pltpu.VMEM((3, width, ff), half),
            pltpu.VMEM((4 * toks, ff), half),
            pltpu.VMEM((4 * toks, LANES), jnp.float32),
            pltpu.VMEM((groups, PIECES, 2, NY, toks, cols), half),
            pltpu.VMEM((groups, PIECES, NY, toks, cols), half),
            pltpu.VMEM((groups, PIECES, toks, cols), half),
            pltpu.VMEM((groups, PIECES, toks, cols), half),
            pltpu.VMEM((groups, PIECES, NY, toks, cols), half),
            pltpu.VMEM((NZ, groups, PIECES, NY, toks, cols), half),
            dma((4,)),
            dma((3,)),
            dma((steps, NZ, 2, NY)),
            dma((steps, NZ, 2, 5)),
            dma((groups, PIECES)),
            dma((groups, PIECES)),
            dma((groups, PIECES)),
            dma((groups, PIECES)),
            dma((NZ, groups, PIECES, NY)),
            dma((groups, PIECES, NY)),
        ],
        compiler_params=pltpu.CompilerParams(
            collective_id=0, has_side_effects=True, vmem_limit_bytes=64 * 1024 * 1024
        ),
        cost_estimate=pl.CostEstimate(
            flops=6 * rows * width * ff, bytes_accessed=6 * width * ff, transcendentals=rows * ff
        ),
    )(
        tokens,
        norm_gain.reshape(1, width),
        expert_ids.transpose(0, 2, 1),
        gate_probs.transpose(0, 2, 1),
        expert_weights,
    )


def solution(mesh):
    in_specs = (
        P(None, ("grp", "ep", "dp"), None),
        P(),
        P(None, ("grp", "ep", "dp"), None),
        P(None, ("grp", "ep", "dp"), None),
        P(("ep", "dp"), None, None, None),
    )
    out_specs = P(None, ("grp", "ep", "dp"), None)
    small = mesh.shape["ep"] == NZ * NY and mesh.shape["dp"] == 2
    shards = kernel_form if small else gather_scatter_form
    return jax.shard_map(shards, mesh=mesh, in_specs=in_specs, out_specs=out_specs, check_vma=False)
```

```python
import functools

import jax
import jax.numpy as jnp
from jax import lax
from jax.experimental import pallas as pl
from jax.experimental.pallas import tpu as pltpu
from jax.sharding import PartitionSpec as P

NZ = 4
NY = 2
LANES = 128
PIECES = 1
F_TILE = 256
LEAPS = 0
DIRECT = 1
ROW = 6
PLANS = (
    (
        1520640, -1340066800, -2147377024, 33620225, -1601142782, 17891345,
        34713664, -1600126958, 2163716, -1336934111, -1598029279, 2229268,
        21037121, -1335885247, 4326436, 5349584, -1334836911, 71565905,
        -1595932590, 673382497, 39911777, 72655088, 675479650, -1339031439,
        40960369, 7472228, 872949843, 807941144, 3252400, 74711345,
        140706353, 545783858, 67707032, 547893320, 141755444, 811074585,
        812130504, 813179096, 552078377, 553126985, 674443320, 548932697,
        1611009129, 209281046, 986169, 983055, 983055, 983055,
    ),
    (
        1520640, -1340066800, -2147376000, -1534066431, -1337982463, 1146882,
        17932448, 34709584, 1220800, 2163732, 35717409, 2269280,
        606273601, 21045411, 37855440, -1603272638, 549659715, 22085713,
        38904032, -1594884014, 6358100, 39911777, 6463536, 7415891,
        14877795, 24223920, 7471729, 74724360, 807941144, 19988529,
        3277361, 612894835, 70526104, 547893320, 542639129, 405348552,
        551034984, 544741449, 553132264, 540544089, 674437225, 548955269,
        209281046, 205086726, 984073, 983055, 983055, 983055,
    ),
    (
        3619872, -1275055056, -1600079808, 18972705, -2145254879, -1273978704,
        3258448, 36766001, -1201627008, 3277860, 106688, -1200619263,
        33661072, 70557904, -1595932670, 21037121, 4325953, 1115140,
        -1594883823, 34670640, 71565330, 671285329, 38863185, 68419666,
        675479649, 39911777, 72613986, 672333937, 40960369, 73662578,
        876100648, 944256008, -802807640, 548939859, 74724376, 69810264,
        946020488, 549992552, 947389497, 551035032, 553132264, 201918520,
        206125171, -801764327, 208211033, 986233, 983055, 983055,
    ),
    (
        3619872, -1543490512, -1600079808, -1531936735, -1471110128, -1535114975,
        -2145254879, -1597987696, 3254368, -1462763215, 3277361, -1469054975,
        16843828, 33663200, -1460666366, 145754160, 545465347, 21037121,
        4325953, 549659715, 17891345, 1180177, 5309460, 38863185,
        72613970, 672388261, 23134305, 6423137, 7415891, 878903665,
        7471729, -802814860, 1009266915, 604517432, 547895368, 605562040,
        612903000, 947070104, 677912776, 70854872, 686303352, 687347721,
        146278456, 69802057, -801764327, 409537625, 986233, 983055,
    ),
    (
        5717056, -1201653680, -1597983712, 21069889, -2143157695, -1271881520,
        5355632, 38863185, -1275027232, 5375044, 2203808, -1274019551,
        35758256, 72655088, -1602224094, 23134305, 6423137, 3212388,
        -1601175247, 36766800, 69468210, 677576817, 40960369, 70516850,
        673382401, 33620225, 74711042, 674430993, 34668817, 67371026,
        -1337574328, 946354264, 678638632, 551035080, 68432952, 71907448,
        939729128, 547894280, 873989209, 553132216, 546840712, 208208984,
        204027923, -1336538055, 201919609, 986137, 983055, 983055,
    ),
    (
        5717056, -1470089136, -1597983712, -1462730687, -1469012944, -1461714623,
        -2143157695, -1600083728, 5350400, 38863185, 5416112, -1542455199,
        23135316, 39953536, -1534066590, 80741456, 18939937, 2228769,
        610477091, 551755939, 19988529, 3277361, 7406644, 40960369,
        74711154, 674477253, 16842753, 131585, 1124467, 872612113,
        1180177, -1337588716, 1011363971, 677918808, 549991464, 607660248,
        686303352, 940779768, 604512424, 72950968, 612901912, 72885400,
        405341400, 71899241, -1336538055, 403246201, 986137, 983055,
    ),
    (
        7813216, -1337968528, -2141085472, 39911777, -1594851230, 24182897,
        41005088, -1598029710, 4260964, -1339031231, -1600126399, 4326516,
        18939937, -1342176735, 2229316, 3252400, -1341128399, 69468721,
        -1602224078, 675479553, 33620225, 70557840, 673382402, -1336934383,
        34668817, 1180676, 946350131, 810039416, 5349584, 68419921,
        134414929, 552075346, 73998584, 549990440, 135464020, 808977529,
        805839016, 806887608, 545786953, 546835497, 676540504, 551029817,
        1617300489, 1618349081, 986201, 983055, 983055, 983055,
    ),
    (
        7813216, -1337968528, -2141083424, -1460666015, -1340079519, 7438434,
        24223936, 41001008, 7512224, 4260980, 37814593, 4366336,
        608370721, 18948291, 35758256, -1609564126, 547562531, 19988529,
        36806784, -1601175502, 66612, 33620225, 172112, 1124403,
        8586243, 17932496, 1180177, 68434024, 810039416, 22085713,
        5374545, 686295059, 72624376, 549990440, 540542073, 407445672,
        548937736, 538449961, 546840712, 542641209, 676534281, 551052517,
        1617322102, 207162393, 984169, 983055, 983055, 983055,
    ),
)


def norm_rows(hidden_rows, norm_gain):
    values = hidden_rows.astype(jnp.float32)
    inverse_rms = lax.rsqrt(jnp.mean(values * values, axis=-1, keepdims=True) + 1e-06)
    return (values * inverse_rms * norm_gain).astype(jnp.bfloat16)


def expert_rows(row_block, weights):
    gate_part = jnp.dot(row_block, weights[0], preferred_element_type=jnp.float32)
    up_part = jnp.dot(row_block, weights[1], preferred_element_type=jnp.float32)
    hidden = (jax.nn.silu(gate_part) * up_part).astype(jnp.bfloat16)
    return lax.dot_general(
        hidden, weights[2], (((1,), (1,)), ((), ())), preferred_element_type=jnp.float32
    )


def gather_scatter_form(tokens, norm_gain, expert_ids, gate_probs, expert_weights):
    axes = ("ep", "dp")
    experts = lax.axis_size("ep") * lax.axis_size("dp")
    me = lax.axis_index(axes)
    steps_total, tok_count, width = tokens.shape
    rows = steps_total * tok_count
    normed = norm_rows(tokens.reshape(rows, width), norm_gain)
    share = gate_probs / jnp.sum(gate_probs, axis=-1, keepdims=True)
    hits = expert_ids[..., None] == lax.broadcasted_iota(jnp.int32, (1, 1, 1, experts), 3)
    dense_share = jnp.sum(jnp.where(hits, share[..., None], 0.0), axis=2).reshape(rows, experts)
    all_rows = lax.all_gather(normed, axes, tiled=True)
    all_share = lax.all_gather(dense_share, axes, tiled=True)
    mine = lax.broadcasted_iota(jnp.int32, (1, experts), 1) == me
    row_share = jnp.sum(jnp.where(mine, all_share, 0.0), axis=1, keepdims=True)
    expert_out = expert_rows(all_rows, expert_weights[0])
    weighted = (row_share * expert_out).astype(jnp.bfloat16)
    combined = lax.psum_scatter(weighted, axes, scatter_dimension=0, tiled=True)
    return combined.reshape(steps_total, tok_count, width)


def moe_kernel(
    tok_hbm, gain_hbm, ids_hbm, prob_hbm, w_hbm, out_ref,
    tok, gain, ids, prob, x, wv, hid, scale, ob, sr, ys, yr, zs, zr,
    in_sem, w_sem, x_recv, x_send, c_recv, c_send, y_recv, y_send, z_recv, z_send,
):
    steps, toks, width = tok.shape
    top = ids.shape[1]
    ff = wv.shape[2]
    cols = width // PIECES
    experts = lax.axis_size("ep") * lax.axis_size("dp")
    ep = lax.axis_index("ep")
    c = lax.axis_index("dp")
    z = ep // NY
    y = ep % NY
    me = ep * 2 + c

    sib = {"ep": ep, "dp": 1 - c}
    ynb = {"ep": z * NY + 1 - y, "dp": c}
    zup = {"ep": (z + 1) % NZ * NY + y, "dp": c}
    zdn = {"ep": (z + NZ - 1) % NZ * NY + y, "dp": c}
    zfar = {"ep": (NZ - 1 - z) * NY + y, "dp": c}
    can_up = z < NZ - 1
    can_dn = z > 0
    outer = (z == 0) | (z == NZ - 1)

    barrier = pltpu.get_barrier_semaphore()
    for peer in (sib, ynb):
        pl.semaphore_signal(barrier, inc=1, device_id=peer)

    @pl.when(can_up)
    def _():
        pl.semaphore_signal(barrier, inc=1, device_id=zup)

    @pl.when(can_dn)
    def _():
        pl.semaphore_signal(barrier, inc=1, device_id=zdn)

    if LEAPS:
        @pl.when(outer)
        def _():
            pl.semaphore_signal(barrier, inc=1, device_id=zfar)

    loads = [
        pltpu.make_async_copy(tok_hbm, tok, in_sem.at[0]),
        pltpu.make_async_copy(gain_hbm, gain, in_sem.at[1]),
        pltpu.make_async_copy(ids_hbm, ids, in_sem.at[2]),
        pltpu.make_async_copy(prob_hbm, prob, in_sem.at[3]),
    ]
    for load in loads:
        load.start()
    for i in range(3):
        pltpu.make_async_copy(w_hbm.at[0, i], wv.at[i], w_sem.at[i]).start()

    def choose(values, index):
        value = jnp.int32(values[0])
        for place in range(1, len(values)):
            value = jnp.where(index == place, jnp.int32(values[place]), value)
        return value

    words = [choose(column, 2 * z + c) for column in zip(*PLANS)]

    for load in loads:
        load.wait()

    def norm(s):
        x[s, z, c, y, :, :width] = norm_rows(tok[s], gain[...])

    def shares(s):
        probs = prob[s]
        share = probs / jnp.sum(probs, axis=0, keepdims=True)
        named = ids[s]
        row = lax.broadcasted_iota(jnp.int32, (2 * experts, toks), 0)
        both = jnp.zeros((2 * experts, toks), jnp.float32)
        for i in range(top):
            hit = (row == named[i : i + 1]) | (row == named[i : i + 1] + experts)
            both = jnp.where(hit, share[i : i + 1], both)
        high = both.astype(jnp.bfloat16).astype(jnp.float32)
        pieces = jnp.where(row < experts, high, both - high).astype(jnp.bfloat16)
        eye = (
            lax.broadcasted_iota(jnp.int32, (2 * experts, LANES), 0) + 2 * experts * s
            == lax.broadcasted_iota(jnp.int32, (2 * experts, LANES), 1)
        ).astype(jnp.float32).astype(jnp.bfloat16)
        return lax.dot_general(
            pieces, eye, (((0,), (0,)), ((), ())), preferred_element_type=jnp.float32
        )

    norm(0)
    x[0, z, c, y, :, width:] = (shares(0) + shares(1)).astype(jnp.bfloat16)
    peers = 2 + jnp.where(can_up, 1, 0) + jnp.where(can_dn, 1, 0)
    if LEAPS:
        peers = peers + jnp.where(outer, 1, 0)
    pl.semaphore_wait(barrier, peers)

    def x_copy(s, k, col, row, far, act, do):
        peer = (zup, zdn, ynb, sib, zfar)[act]
        for block, here in (
            (x.at[s, k, col, row], s == 0),
            (x.at[s, k, col, row, :, :width], s > 0),
        ):
            @pl.when(here)
            def _(block=block):
                do(pltpu.make_async_remote_copy(
                    block, block, x_send.at[s, k, far, act], x_recv.at[s, k, col, row],
                    device_id=peer,
                ))

    def c_copy(n, p):
        return pltpu.make_async_remote_copy(
            ob.at[n, p, 1 - c], sr.at[n, p], c_send.at[n, p], c_recv.at[n, p], device_id=sib
        )

    def y_copy(n, p):
        return pltpu.make_async_remote_copy(
            ys.at[n, p], yr.at[n, p], y_send.at[n, p], y_recv.at[n, p], device_id=ynb
        )

    def z_copy(n, p, far, source, target):
        return pltpu.make_async_remote_copy(
            zs.at[n, p, far], zr.at[source, n, p, far], z_send.at[n, p, far],
            z_recv.at[source, n, p, far], device_id={"ep": target * NY + y, "dp": c},
        )

    def start(copy):
        copy.start()

    def sent(copy):
        copy.wait_send()

    def got(copy):
        copy.wait_recv()

    def f32(value):
        return value.astype(jnp.float32)

    def do_relay(s, k, far, p, bits):
        row = jnp.where(far == 1, 1 - y, y)

        @pl.when(bits >= 32)
        def _():
            x_copy(s, k, c, row, far, 2, got)

        for act in range(4 + LEAPS):
            @pl.when(bits // 2**act % 2 == 1)
            def _(act=act):
                x_copy(s, k, c, row, far, act, start)

    def do_sent(s, k, far, p, bits):
        row = jnp.where(far == 1, 1 - y, y)
        for act in range(4 + LEAPS):
            @pl.when(bits // 2**act % 2 == 1)
            def _(act=act):
                x_copy(s, k, c, row, far, act, sent)

    def do_norm(s, k, far, p, bits):
        norm(1)

    def do_hidden(s, k, far, p, bits):
        @pl.when(bits >= 32)
        def _():
            for i in range(2):
                pltpu.make_async_copy(w_hbm.at[0, i], wv.at[i], w_sem.at[i]).wait()

        @pl.when(p == 0)
        def _():
            for row in range(NY):
                x_copy(s, k, 1 - c, row, 0, 3, got)

            rows = 4 * toks
            lane = lax.broadcasted_iota(jnp.int32, (rows, LANES), 1) - 2 * experts * s
            parts = f32(x[0, k, :, :, :, width:].reshape(rows, LANES))
            mine = (lane == me) | (lane == me + experts)
            share = jnp.sum(jnp.where(mine, parts, 0.0), axis=1, keepdims=True)
            scale[...] = jnp.broadcast_to(share, (rows, LANES))

        block = x[s, k, :, :, :, :width].reshape(4 * toks, width)
        here = pl.ds(pl.multiple_of(p * F_TILE, F_TILE), F_TILE)
        gate = jnp.dot(block, wv[0, :, here], preferred_element_type=jnp.float32)
        up = jnp.dot(block, wv[1, :, here], preferred_element_type=jnp.float32)
        hid[:, here] = (gate / (1.0 + jnp.exp(-gate)) * up).astype(jnp.bfloat16)

    def do_out(s, k, far, p, bits):
        @pl.when(bits >= 32)
        def _():
            pltpu.make_async_copy(w_hbm.at[0, 2], wv.at[2], w_sem.at[2]).wait()

        n = s * NZ + k
        hidden = hid[...]
        tile = 256
        share = jnp.concatenate([scale[...]] * (tile // LANES), axis=1)
        for d in range(0, cols, tile):
            part = lax.dot_general(
                hidden, wv[2, pl.ds(pl.multiple_of(p * cols + d, tile), tile), :],
                (((1,), (1,)), ((), ())), preferred_element_type=jnp.float32,
            )
            ob[n, p, :, :, :, d : d + tile] = (
                (share * part).astype(jnp.bfloat16).reshape(2, NY, toks, tile)
            )
        c_copy(n, p).start()

    def pair(n, p, row):
        return f32(ob[n, p, c, row]) + f32(sr[n, p, row])

    def first_waits(n, p, bits):
        @pl.when(bits % 2 == 1)
        def _():
            c_copy(n, p).wait_recv()

        @pl.when(bits // 2 % 2 == 1)
        def _():
            y_copy(n, p).wait_recv()

    def do_cross(s, k, far, p, bits):
        n = s * NZ + k
        first_waits(n, p, bits)
        ys[n, p] = pair(n, p, 1 - y).astype(jnp.bfloat16)
        y_copy(n, p).start()

    def do_pass(s, k, far, p, bits):
        n = s * NZ + k
        row = jnp.where(far == 1, 1 - y, y)
        first_waits(n, p, bits)

        step = jnp.where(k > z, 1, -1)
        before = jnp.clip(z - step, 0, NZ - 1)

        @pl.when(bits // 4 % 2 == 1)
        def _():
            z_copy(n, p, far, before, z).wait_recv()

        @pl.when(bits // 2 % 4 == 3)
        def _():
            zs[n, p, far] = (
                pair(n, p, row) + f32(yr[n, p]) + f32(zr[before, n, p, far])
            ).astype(jnp.bfloat16)

        @pl.when(bits // 2 % 4 == 2)
        def _():
            zs[n, p, far] = (pair(n, p, row) + f32(zr[before, n, p, far])).astype(jnp.bfloat16)

        @pl.when(bits // 2 % 4 == 1)
        def _():
            zs[n, p, far] = (pair(n, p, row) + f32(yr[n, p])).astype(jnp.bfloat16)

        @pl.when(bits // 2 % 4 == 0)
        def _():
            zs[n, p, far] = pair(n, p, row).astype(jnp.bfloat16)

        @pl.when(bits // 8 % 2 == 0)
        def _():
            z_copy(n, p, far, z, z + step).start()

        if DIRECT:
            @pl.when(bits // 8 % 2 == 1)
            def _():
                z_copy(n, p, far, z, k).start()

    def arrived(n, p, far, row, bits):
        total = pair(n, p, row)
        for source in range(NZ):
            named = bits // (4 * 2**source) % 2 == 1

            @pl.when(named)
            def _(source=source):
                z_copy(n, p, far, source, (z + 1) % NZ).wait_recv()

            total = total + jnp.where(named, f32(zr[source, n, p, far]), 0.0)
        return total

    def do_hand(s, k, far, p, bits):
        n = s * NZ + k
        first_waits(n, p, bits % 2)
        ys[n, p] = arrived(n, p, 1, 1 - y, bits).astype(jnp.bfloat16)
        y_copy(n, p).start()

    def do_final(s, k, far, p, bits):
        n = s * NZ + k
        first_waits(n, p, bits % 2 + 2)
        total = arrived(n, p, 0, y, bits) + f32(yr[n, p])
        here = pl.ds(pl.multiple_of(p * cols, cols), cols)
        out_ref[s, :, here] = total.astype(jnp.bfloat16)

    def do_settle(s, k, far, p, bits):
        n = s * NZ + k
        c_copy(n, p).wait_send()

        @pl.when(bits % 2 == 1)
        def _():
            y_copy(n, p).wait_send()

        for lane in range(2):
            @pl.when(bits // (2 + 2 * lane) % 2 == 1)
            def _(lane=lane):
                z_copy(n, p, lane, z, (z + 1) % NZ).wait_send()

    kinds = (
        (do_relay, do_hidden, do_out),
        (do_pass, do_cross, do_hand, do_final),
        (do_norm, do_sent, do_settle),
    )

    def obey(code):
        kind = code % 16
        s = code // 16 % 2
        k = code // 32 % 4
        far = code // 128 % 2
        p = code // 256 % 4
        bits = code // 1024
        first = 0
        for some in kinds:
            @pl.when((kind >= first) & (kind < first + len(some)))
            def _(first=first, some=some):
                for number, body in enumerate(some):
                    @pl.when(kind == first + number)
                    def _(body=body):
                        body(s, k, far, p, bits)

            first += len(some)

    blocks = len(words) // ROW

    def block(b, carry):
        row = [choose(words[j::ROW], b) for j in range(ROW)]

        def entry(i, carry):
            word = choose(row, i // 2)
            obey(jnp.where(i % 2 == 0, word & 65535, (word >> 16) & 65535))
            return carry

        lax.fori_loop(0, 2 * ROW, entry, 0)
        return carry

    lax.fori_loop(0, blocks, block, 0)


def kernel_form(tokens, norm_gain, expert_ids, gate_probs, expert_weights):
    steps, toks, width = tokens.shape
    top = expert_ids.shape[2]
    ff = expert_weights.shape[3]
    groups = steps * NZ
    cols = width // PIECES
    half = jnp.bfloat16
    hbm = pl.BlockSpec(memory_space=pltpu.MemorySpace.HBM)
    dma = pltpu.SemaphoreType.DMA
    rows = groups * 4 * toks
    return pl.pallas_call(
        moe_kernel,
        out_shape=jax.ShapeDtypeStruct((steps, toks, width), half),
        in_specs=[hbm, hbm, hbm, hbm, hbm],
        out_specs=pl.BlockSpec(memory_space=pltpu.VMEM),
        scratch_shapes=[
            pltpu.VMEM((steps, toks, width), half),
            pltpu.VMEM((1, width), jnp.float32),
            pltpu.VMEM((steps, top, toks), jnp.int32),
            pltpu.VMEM((steps, top, toks), jnp.float32),
            pltpu.VMEM((steps, NZ, 2, NY, toks, width + LANES), half),
            pltpu.VMEM((3, width, ff), half),
            pltpu.VMEM((4 * toks, ff), half),
            pltpu.VMEM((4 * toks, LANES), jnp.float32),
            pltpu.VMEM((groups, PIECES, 2, NY, toks, cols), half),
            pltpu.VMEM((groups, PIECES, NY, toks, cols), half),
            pltpu.VMEM((groups, PIECES, toks, cols), half),
            pltpu.VMEM((groups, PIECES, toks, cols), half),
            pltpu.VMEM((groups, PIECES, NY, toks, cols), half),
            pltpu.VMEM((NZ, groups, PIECES, NY, toks, cols), half),
            dma((4,)),
            dma((3,)),
            dma((steps, NZ, 2, NY)),
            dma((steps, NZ, 2, 5)),
            dma((groups, PIECES)),
            dma((groups, PIECES)),
            dma((groups, PIECES)),
            dma((groups, PIECES)),
            dma((NZ, groups, PIECES, NY)),
            dma((groups, PIECES, NY)),
        ],
        compiler_params=pltpu.CompilerParams(
            collective_id=0, has_side_effects=True, vmem_limit_bytes=64 * 1024 * 1024
        ),
        cost_estimate=pl.CostEstimate(
            flops=6 * rows * width * ff, bytes_accessed=6 * width * ff, transcendentals=rows * ff
        ),
    )(
        tokens,
        norm_gain.reshape(1, width),
        expert_ids.transpose(0, 2, 1),
        gate_probs.transpose(0, 2, 1),
        expert_weights,
    )


def solution(mesh):
    in_specs = (
        P(None, ("grp", "ep", "dp"), None),
        P(),
        P(None, ("grp", "ep", "dp"), None),
        P(None, ("grp", "ep", "dp"), None),
        P(("ep", "dp"), None, None, None),
    )
    out_specs = P(None, ("grp", "ep", "dp"), None)
    small = mesh.shape["ep"] == NZ * NY and mesh.shape["dp"] == 2
    shards = kernel_form if small else gather_scatter_form
    return jax.shard_map(shards, mesh=mesh, in_specs=in_specs, out_specs=out_specs, check_vma=False)
```

```python
import functools

import jax
import jax.numpy as jnp
from jax import lax
from jax.experimental import pallas as pl
from jax.experimental.pallas import tpu as pltpu
from jax.sharding import PartitionSpec as P

NZ = 4
NY = 2
LANES = 128
PIECES = 1
F_TILE = 768
LEAPS = 0
DIRECT = 1
PAIRS = 0
ROW = 6
PLANS = (
    (
        1520640, -1340066800, -2147377024, -1601142782, -1337982959, 1180676,
        2203808, 2229268, -1597984688, 4325441, 69513312, 874001416,
        545796136, 67707032, -1334796080, 5309508, 5415136, 6367267,
        72655088, 675479650, 7450672, 7472228, 68759624, 811081896,
        74721363, 812130504, -1599069992, 140705841, 813170738, 552078377,
        553126985, 70518899, 674443320, 1611009113, 548932713, 209281046,
        986169, 983055, 983055, 983055, 983055, 983055,
    ),
    (
        1520640, -1340066800, -2147376000, -1337940848, 1146882, 1220768,
        872980672, 68432920, 2203728, 606273570, 547594336, 4325441,
        608411856, 807936195, -1603263352, 5317784, 5415136, -1594883999,
        6423636, -1607466895, 14877795, -1599078286, 810035283, 74719400,
        549979161, 405348440, 407445608, 544743640, 3276849, 552077427,
        553124916, 1686444137, 207169587, 548937784, 1611030550, 67701881,
        986169, 983055, 983055, 983055, 983055, 983055,
    ),
    (
        3619872, -1275055056, -1600079808, -2145222623, -1273978704, 3258448,
        -1602224078, 69515360, -1601175551, -1597982608, 132148, 4301008,
        -1595932606, 1115140, -1594884078, 71567408, 5374033, 68429827,
        675479649, 72613986, 672333937, 73662578, 876100648, 944256008,
        548937896, 945304600, 74721363, 69849126, 946348168, 546833465,
        549992568, 552083672, 137896184, 206113801, 202979427, 207173747,
        208261174, 986233, 983055, 983055, 983055, 983055,
    ),
    (
        3619872, -1543490512, -1600079808, -1531936735, -1471110128, -2145213312,
        -1470062400, -1534066639, -1462763470, 66612, 174192, 4303072,
        137406704, 604178608, 4333699, 549659715, 1179665, 5309460,
        72613970, -727383967, 6432787, 676528241, 74711154, -802802589,
        876100648, 944251912, 616046760, 820192280, 612903000, 677912776,
        613942329, 678963416, 403253480, 137898232, 146282569, 947061801,
        207162393, 409587766, 986233, 983055, 983055, 983055,
    ),
    (
        5717056, -1201653680, -1597983712, -2143125439, -1271881520, 5355632,
        -1595932590, 71611392, -1274019743, -1600085840, 6423636, 2203888,
        -1602224094, 3212388, -1601175502, 69469264, 7471217, 70527075,
        673382401, 74711042, 674430993, 67371026, 945306696, 875051112,
        551035080, 876130374, 68429939, 71907448, 872947944, 873989209,
        547889336, 545792248, 72884376, 204016745, 205076483, 209270803,
        201961558, 986137, 983055, 983055, 983055, 983055,
    ),
    (
        5717056, -1470089136, -1597983712, -1462730687, -1469012944, -2143115040,
        -1543462752, -1460666287, -1531969454, 6358100, 6464528, 2204800,
        72393872, 610469072, 2236643, 547562531, 3276849, 7406644,
        74711154, -1262157823, 141363, 678625297, 68419602, -1337576445,
        945306696, 875047016, 685252808, 813900856, 686303352, 604512424,
        687342681, 605562040, 409543816, 72885400, 81270825, 940770377,
        209259577, 403288150, 986137, 983055, 983055, 983055,
    ),
    (
        7813216, -1337968528, -2141085472, -1594851230, -1340080015, 7472228,
        4300992, -1339030412, -1600126910, 2228257, 71610368, 947402856,
        552087624, 73998584, -1341087568, 3212324, 3317888, 75843,
        70557840, 673382402, 1159248, 1180676, 75051048, 808984776,
        68429875, 805839016, -1596972872, 134414417, 806879314, 545786953,
        546835497, 72615955, 676540504, 201919545, 1617305816, 1618349081,
        986201, 983055, 983055, 983055, 983055, 983055,
    ),
    (
        7813216, -1337968528, -2141083424, -1340036880, 7438434, 7512256,
        946380960, -1607452552, 4260980, -1610612670, 549659715, 2228257,
        606314672, 810033315, 686333968, 3221752, 3317888, 106640,
        132148, 1155152, 8586243, -1596981230, 807938099, 68427976,
        547882105, 407445560, 405348360, 538452152, 5374033, 545785875,
        546833492, 542644233, 205072467, 1692737752, 202989686, 207183974,
        984169, 983055, 983055, 983055, 983055, 983055,
    ),
)


def norm_rows(hidden_rows, norm_gain):
    values = hidden_rows.astype(jnp.float32)
    inverse_rms = lax.rsqrt(jnp.mean(values * values, axis=-1, keepdims=True) + 1e-06)
    return (values * inverse_rms * norm_gain).astype(jnp.bfloat16)


def expert_rows(row_block, weights):
    gate_part = jnp.dot(row_block, weights[0], preferred_element_type=jnp.float32)
    up_part = jnp.dot(row_block, weights[1], preferred_element_type=jnp.float32)
    hidden = (jax.nn.silu(gate_part) * up_part).astype(jnp.bfloat16)
    return lax.dot_general(
        hidden, weights[2], (((1,), (1,)), ((), ())), preferred_element_type=jnp.float32
    )


def gather_scatter_form(tokens, norm_gain, expert_ids, gate_probs, expert_weights):
    axes = ("ep", "dp")
    experts = lax.axis_size("ep") * lax.axis_size("dp")
    me = lax.axis_index(axes)
    steps_total, tok_count, width = tokens.shape
    rows = steps_total * tok_count
    normed = norm_rows(tokens.reshape(rows, width), norm_gain)
    share = gate_probs / jnp.sum(gate_probs, axis=-1, keepdims=True)
    hits = expert_ids[..., None] == lax.broadcasted_iota(jnp.int32, (1, 1, 1, experts), 3)
    dense_share = jnp.sum(jnp.where(hits, share[..., None], 0.0), axis=2).reshape(rows, experts)
    all_rows = lax.all_gather(normed, axes, tiled=True)
    all_share = lax.all_gather(dense_share, axes, tiled=True)
    mine = lax.broadcasted_iota(jnp.int32, (1, experts), 1) == me
    row_share = jnp.sum(jnp.where(mine, all_share, 0.0), axis=1, keepdims=True)
    expert_out = expert_rows(all_rows, expert_weights[0])
    weighted = (row_share * expert_out).astype(jnp.bfloat16)
    combined = lax.psum_scatter(weighted, axes, scatter_dimension=0, tiled=True)
    return combined.reshape(steps_total, tok_count, width)


def moe_kernel(
    tok_hbm, gain_hbm, ids_hbm, prob_hbm, w_hbm, out_ref,
    tok, gain, ids, prob, x, wv, hid, scale, ob, sr, ys, yr, zs, zr,
    in_sem, w_sem, x_recv, x_send, c_recv, c_send, y_recv, y_send, z_recv, z_send,
):
    steps, toks, width = tok.shape
    group = 4 * toks
    top = ids.shape[1]
    ff = wv.shape[2]
    cols = width // PIECES
    experts = lax.axis_size("ep") * lax.axis_size("dp")
    ep = lax.axis_index("ep")
    c = lax.axis_index("dp")
    z = ep // NY
    y = ep % NY
    me = ep * 2 + c

    sib = {"ep": ep, "dp": 1 - c}
    ynb = {"ep": z * NY + 1 - y, "dp": c}
    zup = {"ep": (z + 1) % NZ * NY + y, "dp": c}
    zdn = {"ep": (z + NZ - 1) % NZ * NY + y, "dp": c}
    zfar = {"ep": (NZ - 1 - z) * NY + y, "dp": c}
    can_up = z < NZ - 1
    can_dn = z > 0
    outer = (z == 0) | (z == NZ - 1)

    barrier = pltpu.get_barrier_semaphore()
    for peer in (sib, ynb):
        pl.semaphore_signal(barrier, inc=1, device_id=peer)

    @pl.when(can_up)
    def _():
        pl.semaphore_signal(barrier, inc=1, device_id=zup)

    @pl.when(can_dn)
    def _():
        pl.semaphore_signal(barrier, inc=1, device_id=zdn)

    if LEAPS:
        @pl.when(outer)
        def _():
            pl.semaphore_signal(barrier, inc=1, device_id=zfar)

    loads = [
        pltpu.make_async_copy(tok_hbm, tok, in_sem.at[0]),
        pltpu.make_async_copy(gain_hbm, gain, in_sem.at[1]),
        pltpu.make_async_copy(ids_hbm, ids, in_sem.at[2]),
        pltpu.make_async_copy(prob_hbm, prob, in_sem.at[3]),
    ]
    for load in loads:
        load.start()
    for i in range(3):
        pltpu.make_async_copy(w_hbm.at[0, i], wv.at[i], w_sem.at[i]).start()

    def choose(values, index):
        value = jnp.int32(values[0])
        for place in range(1, len(values)):
            value = jnp.where(index == place, jnp.int32(values[place]), value)
        return value

    words = [choose(column, 2 * z + c) for column in zip(*PLANS)]

    for load in loads:
        load.wait()

    def norm(s):
        x[s, z, c, y, :, :width] = norm_rows(tok[s], gain[...])

    def shares(s):
        probs = prob[s]
        share = probs / jnp.sum(probs, axis=0, keepdims=True)
        named = ids[s]
        row = lax.broadcasted_iota(jnp.int32, (2 * experts, toks), 0)
        both = jnp.zeros((2 * experts, toks), jnp.float32)
        for i in range(top):
            hit = (row == named[i : i + 1]) | (row == named[i : i + 1] + experts)
            both = jnp.where(hit, share[i : i + 1], both)
        high = both.astype(jnp.bfloat16).astype(jnp.float32)
        pieces = jnp.where(row < experts, high, both - high).astype(jnp.bfloat16)
        eye = (
            lax.broadcasted_iota(jnp.int32, (2 * experts, LANES), 0) + 2 * experts * s
            == lax.broadcasted_iota(jnp.int32, (2 * experts, LANES), 1)
        ).astype(jnp.float32).astype(jnp.bfloat16)
        return lax.dot_general(
            pieces, eye, (((0,), (0,)), ((), ())), preferred_element_type=jnp.float32
        )

    norm(0)
    x[0, z, c, y, :, width:] = (shares(0) + shares(1)).astype(jnp.bfloat16)
    peers = 2 + jnp.where(can_up, 1, 0) + jnp.where(can_dn, 1, 0)
    if LEAPS:
        peers = peers + jnp.where(outer, 1, 0)
    pl.semaphore_wait(barrier, peers)

    def x_copy(s, k, col, row, far, act, do):
        peer = (zup, zdn, ynb, sib, zfar)[act]
        for block, here in (
            (x.at[s, k, col, row], s == 0),
            (x.at[s, k, col, row, :, :width], s > 0),
        ):
            @pl.when(here)
            def _(block=block):
                do(pltpu.make_async_remote_copy(
                    block, block, x_send.at[s, k, far, act], x_recv.at[s, k, col, row],
                    device_id=peer,
                ))

    def c_copy(n, p):
        return pltpu.make_async_remote_copy(
            ob.at[n, p, 1 - c], sr.at[n, p], c_send.at[n, p], c_recv.at[n, p], device_id=sib
        )

    def y_copy(n, p):
        return pltpu.make_async_remote_copy(
            ys.at[n, p], yr.at[n, p], y_send.at[n, p], y_recv.at[n, p], device_id=ynb
        )

    def z_copy(n, p, far, source, target):
        return pltpu.make_async_remote_copy(
            zs.at[n, p, far], zr.at[source, n, p, far], z_send.at[n, p, far],
            z_recv.at[source, n, p, far], device_id={"ep": target * NY + y, "dp": c},
        )

    def start(copy):
        copy.start()

    def sent(copy):
        copy.wait_send()

    def got(copy):
        copy.wait_recv()

    def f32(value):
        return value.astype(jnp.float32)

    def do_relay(s, k, far, p, bits):
        row = jnp.where(far == 1, 1 - y, y)

        @pl.when(bits >= 32)
        def _():
            x_copy(s, k, c, row, far, 2, got)

        for act in range(4 + LEAPS):
            @pl.when(bits // 2**act % 2 == 1)
            def _(act=act):
                x_copy(s, k, c, row, far, act, start)

    def do_sent(s, k, far, p, bits):
        row = jnp.where(far == 1, 1 - y, y)
        for act in range(4 + LEAPS):
            @pl.when(bits // 2**act % 2 == 1)
            def _(act=act):
                x_copy(s, k, c, row, far, act, sent)

    def do_norm(s, k, far, p, bits):
        norm(1)

    def do_hidden(s, k, far, p, bits):
        @pl.when(bits >= 32)
        def _():
            for i in range(2):
                pltpu.make_async_copy(w_hbm.at[0, i], wv.at[i], w_sem.at[i]).wait()

        @pl.when(p == 0)
        def _():
            for row in range(NY):
                x_copy(s, k, 1 - c, row, 0, 3, got)

        @pl.when(far == 0)
        def _():
            @pl.when(p == 0)
            def _():
                scale[:group] = scales(s, k)

            hidden_part(x[s, k, :, :, :, :width].reshape(group, width), p, group)

        if PAIRS:
            @pl.when(far == 1)
            def _():
                @pl.when(p == 0)
                def _():
                    for row in range(NY):
                        x_copy(1, k, 1 - c, row, 0, 3, got)

                    for q in range(2):
                        scale[q * group : (q + 1) * group] = scales(q, k)

                hidden_part(x[:, k, :, :, :, :width].reshape(2 * group, width), p, 2 * group)

    def scales(s, k):
        lane = lax.broadcasted_iota(jnp.int32, (group, LANES), 1) - 2 * experts * s
        parts = f32(x[0, k, :, :, :, width:].reshape(group, LANES))
        mine = (lane == me) | (lane == me + experts)
        share = jnp.sum(jnp.where(mine, parts, 0.0), axis=1, keepdims=True)
        return jnp.broadcast_to(share, (group, LANES))

    def hidden_part(block, p, rows):
        for f in range(0, F_TILE, 256):
            here = pl.ds(pl.multiple_of(p * F_TILE + f, 256), 256)
            gate = jnp.dot(block, wv[0, :, here], preferred_element_type=jnp.float32)
            up = jnp.dot(block, wv[1, :, here], preferred_element_type=jnp.float32)
            hid[:rows, here] = (gate / (1.0 + jnp.exp(-gate)) * up).astype(jnp.bfloat16)

    def do_out(s, k, far, p, bits):
        @pl.when(bits >= 32)
        def _():
            pltpu.make_async_copy(w_hbm.at[0, 2], wv.at[2], w_sem.at[2]).wait()

        def out_part(rows):
            hidden = hid[:rows]
            tile = 256
            share = jnp.concatenate([scale[:rows]] * (tile // LANES), axis=1)
            for d in range(0, cols, tile):
                part = lax.dot_general(
                    hidden, wv[2, pl.ds(pl.multiple_of(p * cols + d, tile), tile), :],
                    (((1,), (1,)), ((), ())), preferred_element_type=jnp.float32,
                )
                done = (share * part).astype(jnp.bfloat16)
                for q in range(rows // group):
                    ob[(s + q) * NZ + k, p, :, :, :, d : d + tile] = (
                        done[q * group : (q + 1) * group].reshape(2, NY, toks, tile)
                    )
            for q in range(rows // group):
                c_copy((s + q) * NZ + k, p).start()

        @pl.when(far == 0)
        def _():
            out_part(group)

        if PAIRS:
            @pl.when(far == 1)
            def _():
                out_part(2 * group)

    def pair(n, p, row):
        return f32(ob[n, p, c, row]) + f32(sr[n, p, row])

    def first_waits(n, p, bits):
        @pl.when(bits % 2 == 1)
        def _():
            c_copy(n, p).wait_recv()

        @pl.when(bits // 2 % 2 == 1)
        def _():
            y_copy(n, p).wait_recv()

    def do_cross(s, k, far, p, bits):
        n = s * NZ + k
        first_waits(n, p, bits)
        ys[n, p] = pair(n, p, 1 - y).astype(jnp.bfloat16)
        y_copy(n, p).start()

    def do_pass(s, k, far, p, bits):
        n = s * NZ + k
        row = jnp.where(far == 1, 1 - y, y)
        first_waits(n, p, bits)

        step = jnp.where(k > z, 1, -1)
        before = jnp.clip(z - step, 0, NZ - 1)

        @pl.when(bits // 4 % 2 == 1)
        def _():
            z_copy(n, p, far, before, z).wait_recv()

        @pl.when(bits // 2 % 4 == 3)
        def _():
            zs[n, p, far] = (
                pair(n, p, row) + f32(yr[n, p]) + f32(zr[before, n, p, far])
            ).astype(jnp.bfloat16)

        @pl.when(bits // 2 % 4 == 2)
        def _():
            zs[n, p, far] = (pair(n, p, row) + f32(zr[before, n, p, far])).astype(jnp.bfloat16)

        @pl.when(bits // 2 % 4 == 1)
        def _():
            zs[n, p, far] = (pair(n, p, row) + f32(yr[n, p])).astype(jnp.bfloat16)

        @pl.when(bits // 2 % 4 == 0)
        def _():
            zs[n, p, far] = pair(n, p, row).astype(jnp.bfloat16)

        @pl.when(bits // 8 % 2 == 0)
        def _():
            z_copy(n, p, far, z, z + step).start()

        if DIRECT:
            @pl.when(bits // 8 % 2 == 1)
            def _():
                z_copy(n, p, far, z, k).start()

    def arrived(n, p, far, row, bits):
        total = pair(n, p, row)
        for source in range(NZ):
            named = bits // (4 * 2**source) % 2 == 1

            @pl.when(named)
            def _(source=source):
                z_copy(n, p, far, source, (z + 1) % NZ).wait_recv()

            total = total + jnp.where(named, f32(zr[source, n, p, far]), 0.0)
        return total

    def do_hand(s, k, far, p, bits):
        n = s * NZ + k
        first_waits(n, p, bits % 2)
        ys[n, p] = arrived(n, p, 1, 1 - y, bits).astype(jnp.bfloat16)
        y_copy(n, p).start()

    def do_final(s, k, far, p, bits):
        n = s * NZ + k
        first_waits(n, p, bits % 2 + 2)
        total = arrived(n, p, 0, y, bits) + f32(yr[n, p])
        here = pl.ds(pl.multiple_of(p * cols, cols), cols)
        out_ref[s, :, here] = total.astype(jnp.bfloat16)

    def do_settle(s, k, far, p, bits):
        n = s * NZ + k
        c_copy(n, p).wait_send()

        @pl.when(bits % 2 == 1)
        def _():
            y_copy(n, p).wait_send()

        for lane in range(2):
            @pl.when(bits // (2 + 2 * lane) % 2 == 1)
            def _(lane=lane):
                z_copy(n, p, lane, z, (z + 1) % NZ).wait_send()

    kinds = (
        (do_relay, do_hidden, do_out),
        (do_pass, do_cross, do_hand, do_final),
        (do_norm, do_sent, do_settle),
    )

    def obey(code):
        kind = code % 16
        s = code // 16 % 2
        k = code // 32 % 4
        far = code // 128 % 2
        p = code // 256 % 4
        bits = code // 1024
        first = 0
        for some in kinds:
            @pl.when((kind >= first) & (kind < first + len(some)))
            def _(first=first, some=some):
                for number, body in enumerate(some):
                    @pl.when(kind == first + number)
                    def _(body=body):
                        body(s, k, far, p, bits)

            first += len(some)

    blocks = len(words) // ROW

    def block(b, carry):
        row = [choose(words[j::ROW], b) for j in range(ROW)]

        def entry(i, carry):
            word = choose(row, i // 2)
            obey(jnp.where(i % 2 == 0, word & 65535, (word >> 16) & 65535))
            return carry

        lax.fori_loop(0, 2 * ROW, entry, 0)
        return carry

    lax.fori_loop(0, blocks, block, 0)


def kernel_form(tokens, norm_gain, expert_ids, gate_probs, expert_weights):
    steps, toks, width = tokens.shape
    top = expert_ids.shape[2]
    ff = expert_weights.shape[3]
    groups = steps * NZ
    cols = width // PIECES
    half = jnp.bfloat16
    hbm = pl.BlockSpec(memory_space=pltpu.MemorySpace.HBM)
    dma = pltpu.SemaphoreType.DMA
    rows = groups * 4 * toks
    return pl.pallas_call(
        moe_kernel,
        out_shape=jax.ShapeDtypeStruct((steps, toks, width), half),
        in_specs=[hbm, hbm, hbm, hbm, hbm],
        out_specs=pl.BlockSpec(memory_space=pltpu.VMEM),
        scratch_shapes=[
            pltpu.VMEM((steps, toks, width), half),
            pltpu.VMEM((1, width), jnp.float32),
            pltpu.VMEM((steps, top, toks), jnp.int32),
            pltpu.VMEM((steps, top, toks), jnp.float32),
            pltpu.VMEM((steps, NZ, 2, NY, toks, width + LANES), half),
            pltpu.VMEM((3, width, ff), half),
            pltpu.VMEM((8 * toks, ff), half),
            pltpu.VMEM((8 * toks, LANES), jnp.float32),
            pltpu.VMEM((groups, PIECES, 2, NY, toks, cols), half),
            pltpu.VMEM((groups, PIECES, NY, toks, cols), half),
            pltpu.VMEM((groups, PIECES, toks, cols), half),
            pltpu.VMEM((groups, PIECES, toks, cols), half),
            pltpu.VMEM((groups, PIECES, NY, toks, cols), half),
            pltpu.VMEM((NZ, groups, PIECES, NY, toks, cols), half),
            dma((4,)),
            dma((3,)),
            dma((steps, NZ, 2, NY)),
            dma((steps, NZ, 2, 5)),
            dma((groups, PIECES)),
            dma((groups, PIECES)),
            dma((groups, PIECES)),
            dma((groups, PIECES)),
            dma((NZ, groups, PIECES, NY)),
            dma((groups, PIECES, NY)),
        ],
        compiler_params=pltpu.CompilerParams(
            collective_id=0, has_side_effects=True, vmem_limit_bytes=64 * 1024 * 1024
        ),
        cost_estimate=pl.CostEstimate(
            flops=6 * rows * width * ff, bytes_accessed=6 * width * ff, transcendentals=rows * ff
        ),
    )(
        tokens,
        norm_gain.reshape(1, width),
        expert_ids.transpose(0, 2, 1),
        gate_probs.transpose(0, 2, 1),
        expert_weights,
    )


def solution(mesh):
    in_specs = (
        P(None, ("grp", "ep", "dp"), None),
        P(),
        P(None, ("grp", "ep", "dp"), None),
        P(None, ("grp", "ep", "dp"), None),
        P(("ep", "dp"), None, None, None),
    )
    out_specs = P(None, ("grp", "ep", "dp"), None)
    small = mesh.shape["ep"] == NZ * NY and mesh.shape["dp"] == 2
    shards = kernel_form if small else gather_scatter_form
    return jax.shard_map(shards, mesh=mesh, in_specs=in_specs, out_specs=out_specs, check_vma=False)
```

```python
import functools

import jax
import jax.numpy as jnp
from jax import lax
from jax.experimental import pallas as pl
from jax.experimental.pallas import tpu as pltpu
from jax.sharding import PartitionSpec as P

NZ = 4
NY = 2
LANES = 128
PIECES = 1
F_TILE = 768
LEAPS = 0
DIRECT = 1
PAIRS = 0
ROW = 6
PLANS = (
    (
        1520640, -1340066800, -2147377024, -1601142782, -1337982959, 1180676,
        2203808, 2229268, -1597984688, 4325441, 69513312, 874001416,
        545796136, 67707032, -1596968888, 71610480, -1595932591, 673382482,
        -1594883999, 6423636, -1339021245, 73662577, 68747378, 811081896,
        676536520, 812123252, 813179096, 3252400, 3278947, 552078377,
        553126985, 141766712, 207160372, 674434153, 1611014328, 986233,
        983055, 983055, 983055, 983055, 983055, 205086742,
    ),
    (
        1520640, -1340066800, -2147376000, -1337940848, 1146882, 1220768,
        872980672, 68432920, 2203728, 606273570, 547594336, 4325441,
        608411856, 807936195, -1603263352, 5317784, 5415136, -1594883999,
        6423636, -1607466895, 14877795, -1599078286, 810035283, 74719400,
        549979161, 405348440, 407445608, 544743640, 3276849, 552077427,
        553124916, 207165545, 548937784, 674456709, 1007638, 983055,
        983055, 983055, 983055, 983055, 209281030, 205063177,
    ),
    (
        3619872, -1275055056, -1600079808, -2145222623, -1273978704, 3258448,
        -1602224078, 69515360, -1601175551, -1597982608, 132148, 4301008,
        -1595932606, 1115140, -1594884078, 71567408, 5374033, 68429827,
        675479649, 72613986, 672333937, 73662578, 876100648, 944256008,
        548937896, 945304600, 74721363, 69849126, 946348168, 546833465,
        549992568, 552083672, 137896184, 206113801, 946015257, 947063897,
        986217, 983055, 983055, 983055, 983055, 209309750,
    ),
    (
        3619872, -1543490512, -1600079808, -1531936735, -1471110128, -2145213312,
        -1470062400, -1534066639, -1462763470, 66612, 174192, 4303072,
        137406704, 604178608, 4333699, 549659715, 1179665, 5309460,
        72613970, -727383967, 6432787, 676528241, 74711154, -802802589,
        876100648, 944251912, 616046760, 820192280, 612903000, 677912776,
        613942329, 678963416, 403253480, 137898232, 146282569, 202966057,
        947063897, 989289, 983055, 983055, 983055, 209309750,
    ),
    (
        5717056, -1201653680, -1597983712, -2143125439, -1271881520, 5355632,
        -1595932590, 71611392, -1274019743, -1600085840, 6423636, 2203888,
        -1602224094, 3212388, -1601175502, 69469264, 7471217, 70527075,
        673382401, 74711042, 674430993, 67371026, 945306696, 875051112,
        551035080, 876130374, 68429939, 71907448, 872947944, 873989209,
        547889336, 545792248, 72884376, 204016745, 939723833, 940772473,
        986121, 983055, 983055, 983055, 983055, 203010134,
    ),
    (
        5717056, -1470089136, -1597983712, -1462730687, -1469012944, -2143115040,
        -1543462752, -1460666287, -1531969454, 6358100, 6464528, 2204800,
        72393872, 610469072, 2236643, 547562531, 3276849, 7406644,
        74711154, -1262157823, 141363, 678625297, 68419602, -1337576445,
        945306696, 875047016, 685252808, 813900856, 686303352, 604512424,
        687342681, 605562040, 409543816, 72885400, 81270825, 205063241,
        940772473, 989193, 983055, 983055, 983055, 203010134,
    ),
    (
        7813216, -1337968528, -2141085472, -1594851230, -1340080015, 7472228,
        4300992, -1339030412, -1600126910, 2228257, 71610368, 947402856,
        552087624, 73998584, -1599066072, 69513232, -1602224079, 675479602,
        -1601175551, 132148, -1336924125, 67371025, 75038738, 808984776,
        674439336, 805831700, 806887608, 5349584, 5376003, 545786953,
        546835497, 135475288, 205063252, 676531209, 1617305816, 986137,
        983055, 983055, 983055, 983055, 983055, 207183990,
    ),
    (
        7813216, -1337968528, -2141083424, -1340036880, 7438434, 7512256,
        946380960, -1607452552, 4260980, -1610612670, 549659715, 2228257,
        606314672, 810033315, 686333968, 3221752, 3317888, 106640,
        132148, 1155152, 8586243, -1596981230, 807938099, 68427976,
        547882105, 407445560, 405348360, 538452152, 5374033, 545785875,
        546833492, 542644233, 551029817, 1692739667, 1618349081, 983055,
        983055, 983055, 983055, 983055, 1617297423, 73993305,
    ),
)


def norm_rows(hidden_rows, norm_gain):
    values = hidden_rows.astype(jnp.float32)
    inverse_rms = lax.rsqrt(jnp.mean(values * values, axis=-1, keepdims=True) + 1e-06)
    return (values * inverse_rms * norm_gain).astype(jnp.bfloat16)


def expert_rows(row_block, weights):
    gate_part = jnp.dot(row_block, weights[0], preferred_element_type=jnp.float32)
    up_part = jnp.dot(row_block, weights[1], preferred_element_type=jnp.float32)
    hidden = (jax.nn.silu(gate_part) * up_part).astype(jnp.bfloat16)
    return lax.dot_general(
        hidden, weights[2], (((1,), (1,)), ((), ())), preferred_element_type=jnp.float32
    )


def gather_scatter_form(tokens, norm_gain, expert_ids, gate_probs, expert_weights):
    axes = ("ep", "dp")
    experts = lax.axis_size("ep") * lax.axis_size("dp")
    me = lax.axis_index(axes)
    steps_total, tok_count, width = tokens.shape
    rows = steps_total * tok_count
    normed = norm_rows(tokens.reshape(rows, width), norm_gain)
    share = gate_probs / jnp.sum(gate_probs, axis=-1, keepdims=True)
    hits = expert_ids[..., None] == lax.broadcasted_iota(jnp.int32, (1, 1, 1, experts), 3)
    dense_share = jnp.sum(jnp.where(hits, share[..., None], 0.0), axis=2).reshape(rows, experts)
    all_rows = lax.all_gather(normed, axes, tiled=True)
    all_share = lax.all_gather(dense_share, axes, tiled=True)
    mine = lax.broadcasted_iota(jnp.int32, (1, experts), 1) == me
    row_share = jnp.sum(jnp.where(mine, all_share, 0.0), axis=1, keepdims=True)
    expert_out = expert_rows(all_rows, expert_weights[0])
    weighted = (row_share * expert_out).astype(jnp.bfloat16)
    combined = lax.psum_scatter(weighted, axes, scatter_dimension=0, tiled=True)
    return combined.reshape(steps_total, tok_count, width)


def moe_kernel(
    tok_hbm, gain_hbm, ids_hbm, prob_hbm, w_hbm, out_ref,
    tok, gain, ids, prob, x, wv, hid, scale, ob, sr, ys, yr, zs, zr,
    in_sem, w_sem, x_recv, x_send, c_recv, c_send, y_recv, y_send, z_recv, z_send,
):
    steps, toks, width = tok.shape
    group = 4 * toks
    top = ids.shape[1]
    ff = wv.shape[2]
    cols = width // PIECES
    experts = lax.axis_size("ep") * lax.axis_size("dp")
    ep = lax.axis_index("ep")
    c = lax.axis_index("dp")
    z = ep // NY
    y = ep % NY
    me = ep * 2 + c

    sib = {"ep": ep, "dp": 1 - c}
    ynb = {"ep": z * NY + 1 - y, "dp": c}
    zup = {"ep": (z + 1) % NZ * NY + y, "dp": c}
    zdn = {"ep": (z + NZ - 1) % NZ * NY + y, "dp": c}
    zfar = {"ep": (NZ - 1 - z) * NY + y, "dp": c}
    can_up = z < NZ - 1
    can_dn = z > 0
    outer = (z == 0) | (z == NZ - 1)

    barrier = pltpu.get_barrier_semaphore()
    for peer in (sib, ynb):
        pl.semaphore_signal(barrier, inc=1, device_id=peer)

    @pl.when(can_up)
    def _():
        pl.semaphore_signal(barrier, inc=1, device_id=zup)

    @pl.when(can_dn)
    def _():
        pl.semaphore_signal(barrier, inc=1, device_id=zdn)

    if LEAPS:
        @pl.when(outer)
        def _():
            pl.semaphore_signal(barrier, inc=1, device_id=zfar)

    loads = [
        pltpu.make_async_copy(tok_hbm, tok, in_sem.at[0]),
        pltpu.make_async_copy(gain_hbm, gain, in_sem.at[1]),
        pltpu.make_async_copy(ids_hbm, ids, in_sem.at[2]),
        pltpu.make_async_copy(prob_hbm, prob, in_sem.at[3]),
    ]
    for load in loads:
        load.start()
    for i in range(3):
        pltpu.make_async_copy(w_hbm.at[0, i], wv.at[i], w_sem.at[i]).start()

    def choose(values, index):
        value = jnp.int32(values[0])
        for place in range(1, len(values)):
            value = jnp.where(index == place, jnp.int32(values[place]), value)
        return value

    words = [choose(column, 2 * z + c) for column in zip(*PLANS)]

    for load in loads:
        load.wait()

    def norm(s):
        x[s, z, c, y, :, :width] = norm_rows(tok[s], gain[...])

    def shares(s):
        probs = prob[s]
        share = probs / jnp.sum(probs, axis=0, keepdims=True)
        named = ids[s]
        row = lax.broadcasted_iota(jnp.int32, (2 * experts, toks), 0)
        both = jnp.zeros((2 * experts, toks), jnp.float32)
        for i in range(top):
            hit = (row == named[i : i + 1]) | (row == named[i : i + 1] + experts)
            both = jnp.where(hit, share[i : i + 1], both)
        high = both.astype(jnp.bfloat16).astype(jnp.float32)
        pieces = jnp.where(row < experts, high, both - high).astype(jnp.bfloat16)
        eye = (
            lax.broadcasted_iota(jnp.int32, (2 * experts, LANES), 0) + 2 * experts * s
            == lax.broadcasted_iota(jnp.int32, (2 * experts, LANES), 1)
        ).astype(jnp.float32).astype(jnp.bfloat16)
        return lax.dot_general(
            pieces, eye, (((0,), (0,)), ((), ())), preferred_element_type=jnp.float32
        )

    norm(0)
    x[0, z, c, y, :, width:] = (shares(0) + shares(1)).astype(jnp.bfloat16)
    peers = 2 + jnp.where(can_up, 1, 0) + jnp.where(can_dn, 1, 0)
    if LEAPS:
        peers = peers + jnp.where(outer, 1, 0)
    pl.semaphore_wait(barrier, peers)

    def x_copy(s, k, col, row, far, act, do):
        peer = (zup, zdn, ynb, sib, zfar)[act]
        for block, here in (
            (x.at[s, k, col, row], s == 0),
            (x.at[s, k, col, row, :, :width], s > 0),
        ):
            @pl.when(here)
            def _(block=block):
                do(pltpu.make_async_remote_copy(
                    block, block, x_send.at[s, k, far, act], x_recv.at[s, k, col, row],
                    device_id=peer,
                ))

    def c_copy(n, p):
        return pltpu.make_async_remote_copy(
            ob.at[n, p, 1 - c], sr.at[n, p], c_send.at[n, p], c_recv.at[n, p], device_id=sib
        )

    def y_copy(n, p):
        return pltpu.make_async_remote_copy(
            ys.at[n, p], yr.at[n, p], y_send.at[n, p], y_recv.at[n, p], device_id=ynb
        )

    def z_copy(n, p, far, source, target):
        return pltpu.make_async_remote_copy(
            zs.at[n, p, far], zr.at[source, n, p, far], z_send.at[n, p, far],
            z_recv.at[source, n, p, far], device_id={"ep": target * NY + y, "dp": c},
        )

    def start(copy):
        copy.start()

    def sent(copy):
        copy.wait_send()

    def got(copy):
        copy.wait_recv()

    def f32(value):
        return value.astype(jnp.float32)

    def do_relay(s, k, far, p, bits):
        row = jnp.where(far == 1, 1 - y, y)

        @pl.when(bits >= 32)
        def _():
            x_copy(s, k, c, row, far, 2, got)

        for act in range(4 + LEAPS):
            @pl.when(bits // 2**act % 2 == 1)
            def _(act=act):
                x_copy(s, k, c, row, far, act, start)

    def do_sent(s, k, far, p, bits):
        row = jnp.where(far == 1, 1 - y, y)
        for act in range(4 + LEAPS):
            @pl.when(bits // 2**act % 2 == 1)
            def _(act=act):
                x_copy(s, k, c, row, far, act, sent)

    def do_norm(s, k, far, p, bits):
        norm(1)

    def do_hidden(s, k, far, p, bits):
        @pl.when(bits >= 32)
        def _():
            for i in range(2):
                pltpu.make_async_copy(w_hbm.at[0, i], wv.at[i], w_sem.at[i]).wait()

        @pl.when(p == 0)
        def _():
            for row in range(NY):
                x_copy(s, k, 1 - c, row, 0, 3, got)

        @pl.when(far == 0)
        def _():
            @pl.when(p == 0)
            def _():
                scale[:group] = scales(s, k)

            hidden_part(x[s, k, :, :, :, :width].reshape(group, width), p, group)

        if PAIRS:
            @pl.when(far == 1)
            def _():
                @pl.when(p == 0)
                def _():
                    for row in range(NY):
                        x_copy(1, k, 1 - c, row, 0, 3, got)

                    for q in range(2):
                        scale[q * group : (q + 1) * group] = scales(q, k)

                hidden_part(x[:, k, :, :, :, :width].reshape(2 * group, width), p, 2 * group)

    def scales(s, k):
        lane = lax.broadcasted_iota(jnp.int32, (group, LANES), 1) - 2 * experts * s
        parts = f32(x[0, k, :, :, :, width:].reshape(group, LANES))
        mine = (lane == me) | (lane == me + experts)
        share = jnp.sum(jnp.where(mine, parts, 0.0), axis=1, keepdims=True)
        return jnp.broadcast_to(share, (group, LANES))

    def hidden_part(block, p, rows):
        for f in range(0, F_TILE, 256):
            here = pl.ds(pl.multiple_of(p * F_TILE + f, 256), 256)
            gate = jnp.dot(block, wv[0, :, here], preferred_element_type=jnp.float32)
            up = jnp.dot(block, wv[1, :, here], preferred_element_type=jnp.float32)
            hid[:rows, here] = (gate / (1.0 + jnp.exp(-gate)) * up).astype(jnp.bfloat16)

    def do_out(s, k, far, p, bits):
        @pl.when(bits >= 32)
        def _():
            pltpu.make_async_copy(w_hbm.at[0, 2], wv.at[2], w_sem.at[2]).wait()

        def out_part(rows):
            hidden = hid[:rows]
            tile = 256
            share = jnp.concatenate([scale[:rows]] * (tile // LANES), axis=1)
            for d in range(0, cols, tile):
                part = lax.dot_general(
                    hidden, wv[2, pl.ds(pl.multiple_of(p * cols + d, tile), tile), :],
                    (((1,), (1,)), ((), ())), preferred_element_type=jnp.float32,
                )
                done = (share * part).astype(jnp.bfloat16)
                for q in range(rows // group):
                    ob[(s + q) * NZ + k, p, :, :, :, d : d + tile] = (
                        done[q * group : (q + 1) * group].reshape(2, NY, toks, tile)
                    )
            for q in range(rows // group):
                c_copy((s + q) * NZ + k, p).start()

        @pl.when(far == 0)
        def _():
            out_part(group)

        if PAIRS:
            @pl.when(far == 1)
            def _():
                out_part(2 * group)

    def pair(n, p, row):
        return f32(ob[n, p, c, row]) + f32(sr[n, p, row])

    def first_waits(n, p, bits):
        @pl.when(bits % 2 == 1)
        def _():
            c_copy(n, p).wait_recv()

        @pl.when(bits // 2 % 2 == 1)
        def _():
            y_copy(n, p).wait_recv()

    def do_cross(s, k, far, p, bits):
        n = s * NZ + k
        first_waits(n, p, bits)
        ys[n, p] = pair(n, p, 1 - y).astype(jnp.bfloat16)
        y_copy(n, p).start()

    def do_pass(s, k, far, p, bits):
        n = s * NZ + k
        row = jnp.where(far == 1, 1 - y, y)
        first_waits(n, p, bits)

        step = jnp.where(k > z, 1, -1)
        before = jnp.clip(z - step, 0, NZ - 1)

        @pl.when(bits // 4 % 2 == 1)
        def _():
            z_copy(n, p, far, before, z).wait_recv()

        @pl.when(bits // 2 % 4 == 3)
        def _():
            zs[n, p, far] = (
                pair(n, p, row) + f32(yr[n, p]) + f32(zr[before, n, p, far])
            ).astype(jnp.bfloat16)

        @pl.when(bits // 2 % 4 == 2)
        def _():
            zs[n, p, far] = (pair(n, p, row) + f32(zr[before, n, p, far])).astype(jnp.bfloat16)

        @pl.when(bits // 2 % 4 == 1)
        def _():
            zs[n, p, far] = (pair(n, p, row) + f32(yr[n, p])).astype(jnp.bfloat16)

        @pl.when(bits // 2 % 4 == 0)
        def _():
            zs[n, p, far] = pair(n, p, row).astype(jnp.bfloat16)

        @pl.when(bits // 8 % 2 == 0)
        def _():
            z_copy(n, p, far, z, z + step).start()

        if DIRECT:
            @pl.when(bits // 8 % 2 == 1)
            def _():
                z_copy(n, p, far, z, k).start()

    def arrived(n, p, far, row, bits):
        total = pair(n, p, row)
        for source in range(NZ):
            named = bits // (4 * 2**source) % 2 == 1

            @pl.when(named)
            def _(source=source):
                z_copy(n, p, far, source, (z + 1) % NZ).wait_recv()

            total = total + jnp.where(named, f32(zr[source, n, p, far]), 0.0)
        return total

    def do_hand(s, k, far, p, bits):
        n = s * NZ + k
        first_waits(n, p, bits % 2)
        ys[n, p] = arrived(n, p, 1, 1 - y, bits).astype(jnp.bfloat16)
        y_copy(n, p).start()

    def do_final(s, k, far, p, bits):
        n = s * NZ + k
        first_waits(n, p, bits % 2 + 2)
        total = arrived(n, p, 0, y, bits) + f32(yr[n, p])
        here = pl.ds(pl.multiple_of(p * cols, cols), cols)
        out_ref[s, :, here] = total.astype(jnp.bfloat16)

    def do_settle(s, k, far, p, bits):
        n = s * NZ + k
        c_copy(n, p).wait_send()

        @pl.when(bits % 2 == 1)
        def _():
            y_copy(n, p).wait_send()

        for lane in range(2):
            @pl.when(bits // (2 + 2 * lane) % 2 == 1)
            def _(lane=lane):
                z_copy(n, p, lane, z, (z + 1) % NZ).wait_send()

    kinds = (
        (do_relay, do_hidden, do_out),
        (do_pass, do_cross, do_hand, do_final),
        (do_norm, do_sent, do_settle),
    )

    def obey(code):
        kind = code % 16
        s = code // 16 % 2
        k = code // 32 % 4
        far = code // 128 % 2
        p = code // 256 % 4
        bits = code // 1024
        first = 0
        for some in kinds:
            @pl.when((kind >= first) & (kind < first + len(some)))
            def _(first=first, some=some):
                for number, body in enumerate(some):
                    @pl.when(kind == first + number)
                    def _(body=body):
                        body(s, k, far, p, bits)

            first += len(some)

    blocks = len(words) // ROW

    def block(b, carry):
        row = [choose(words[j::ROW], b) for j in range(ROW)]

        def entry(i, carry):
            word = choose(row, i // 2)
            obey(jnp.where(i % 2 == 0, word & 65535, (word >> 16) & 65535))
            return carry

        lax.fori_loop(0, 2 * ROW, entry, 0)
        return carry

    lax.fori_loop(0, blocks, block, 0)


def kernel_form(tokens, norm_gain, expert_ids, gate_probs, expert_weights):
    steps, toks, width = tokens.shape
    top = expert_ids.shape[2]
    ff = expert_weights.shape[3]
    groups = steps * NZ
    cols = width // PIECES
    half = jnp.bfloat16
    hbm = pl.BlockSpec(memory_space=pltpu.MemorySpace.HBM)
    dma = pltpu.SemaphoreType.DMA
    rows = groups * 4 * toks
    return pl.pallas_call(
        moe_kernel,
        out_shape=jax.ShapeDtypeStruct((steps, toks, width), half),
        in_specs=[hbm, hbm, hbm, hbm, hbm],
        out_specs=pl.BlockSpec(memory_space=pltpu.VMEM),
        scratch_shapes=[
            pltpu.VMEM((steps, toks, width), half),
            pltpu.VMEM((1, width), jnp.float32),
            pltpu.VMEM((steps, top, toks), jnp.int32),
            pltpu.VMEM((steps, top, toks), jnp.float32),
            pltpu.VMEM((steps, NZ, 2, NY, toks, width + LANES), half),
            pltpu.VMEM((3, width, ff), half),
            pltpu.VMEM((8 * toks, ff), half),
            pltpu.VMEM((8 * toks, LANES), jnp.float32),
            pltpu.VMEM((groups, PIECES, 2, NY, toks, cols), half),
            pltpu.VMEM((groups, PIECES, NY, toks, cols), half),
            pltpu.VMEM((groups, PIECES, toks, cols), half),
            pltpu.VMEM((groups, PIECES, toks, cols), half),
            pltpu.VMEM((groups, PIECES, NY, toks, cols), half),
            pltpu.VMEM((NZ, groups, PIECES, NY, toks, cols), half),
            dma((4,)),
            dma((3,)),
            dma((steps, NZ, 2, NY)),
            dma((steps, NZ, 2, 5)),
            dma((groups, PIECES)),
            dma((groups, PIECES)),
            dma((groups, PIECES)),
            dma((groups, PIECES)),
            dma((NZ, groups, PIECES, NY)),
            dma((groups, PIECES, NY)),
        ],
        compiler_params=pltpu.CompilerParams(
            collective_id=0, has_side_effects=True, vmem_limit_bytes=64 * 1024 * 1024
        ),
        cost_estimate=pl.CostEstimate(
            flops=6 * rows * width * ff, bytes_accessed=6 * width * ff, transcendentals=rows * ff
        ),
    )(
        tokens,
        norm_gain.reshape(1, width),
        expert_ids.transpose(0, 2, 1),
        gate_probs.transpose(0, 2, 1),
        expert_weights,
    )


def solution(mesh):
    in_specs = (
        P(None, ("grp", "ep", "dp"), None),
        P(),
        P(None, ("grp", "ep", "dp"), None),
        P(None, ("grp", "ep", "dp"), None),
        P(("ep", "dp"), None, None, None),
    )
    out_specs = P(None, ("grp", "ep", "dp"), None)
    small = mesh.shape["ep"] == NZ * NY and mesh.shape["dp"] == 2
    shards = kernel_form if small else gather_scatter_form
    return jax.shard_map(shards, mesh=mesh, in_specs=in_specs, out_specs=out_specs, check_vma=False)
```

```python
import functools

import jax
import jax.numpy as jnp
from jax import lax
from jax.experimental import pallas as pl
from jax.experimental.pallas import tpu as pltpu
from jax.sharding import PartitionSpec as P

NZ = 4
NY = 2
LANES = 128
PIECES = 1
F_TILE = 768
LEAPS = 0
DIRECT = 1
PAIRS = 0
ROW = 6
PLANS = (
    (
        1520640, -1340066800, -2080268160, 1155216, 67416128, -1600126958,
        68419617, -1336934366, 71409856, 69513312, 874001416, 545796136,
        67707032, -1596968888, 71610480, -1595932591, 673382482, -1594883999,
        6423636, -1339021245, 73662577, 68747378, 811081896, 676536520,
        812123252, 813179096, 3252400, 3278947, 552078377, 553126985,
        141766712, 207160372, 674434153, 1611014328, 986233, 983055,
        983055, 983055, 983055, 983055, 983055, 205086742,
    ),
    (
        1520640, -1340066800, -2147376000, -1337940848, 1146882, 1220768,
        872980672, 68432920, 69312592, -1604312029, 71377059, 608411856,
        807936195, -1603263352, 5317784, 5415136, -1594883999, 6423636,
        -1607466895, 14877795, -1599078286, 810035283, 74719400, 549979161,
        405348440, 407445608, 544743640, 141755441, 70525160, 409542904,
        540544089, 1686446264, 1612064819, 983055, 983055, 983055,
        983055, 983055, 983055, 983055, 209281030, 205063177,
    ),
    (
        3619872, -1275055056, -1600079808, -1599044575, -1202670576, -1602223055,
        69515360, -1601175551, -1597982608, 132148, 71409872, 67412192,
        -1594883055, 71567408, 671286353, 6358036, 6432835, 7406676,
        7481363, 1009255524, 872952888, 547895368, 873996472, 676542552,
        -802814860, 545784873, 70858856, 947396760, 551035080, 553132264,
        201918520, 202968137, 207173731, 208222323, 983055, 983055,
        983055, 983055, 983055, 983055, 983055, 209309750,
    ),
    (
        3619872, -1543490512, -1600079808, -1531936735, -1471110128, -2145213312,
        -1470062400, -1534066639, -1462763470, 66612, 174192, 4303072,
        137406704, 604178608, 4333699, 549659715, 68420625, 72614993,
        -727383967, 6432787, 676528241, 74711154, -802802589, 876100648,
        944251912, 616046760, 820192280, 612903000, 677912776, 613942329,
        678963416, 403253480, 137898232, 146282569, 202966057, 947063897,
        989289, 983055, 983055, 983055, 983055, 209309750,
    ),
    (
        5717056, -1201653680, -1597983712, -1596947391, -1200573392, -1595931567,
        71611392, -1274019743, -1600085840, 6423636, 69312752, 73703552,
        -1601174479, 69469264, 677577841, 66612, 141347, 1115252,
        1189939, 1011352580, 946354264, 549991464, -1337581352, 678638648,
        947389460, 552076361, 72954888, 548942872, 553132200, 546840712,
        208208984, 205065257, 209270787, 201930771, 983055, 983055,
        983055, 983055, 983055, 983055, 983055, 203010134,
    ),
    (
        5717056, -1470089136, -1597983712, -1462730687, -1469012944, -2143115040,
        -1543462752, -1460666287, -1531969454, 6358100, 6464528, 2204800,
        72393872, 610469072, 2236643, 547562531, 70517809, 74712177,
        -1262157823, 141363, 678625297, 68419602, -1337576445, 945306696,
        875047016, 685252808, 813900856, 686303352, 604512424, 687342681,
        605562040, 409543816, 72885400, 81270825, 205063241, 940772473,
        989193, 983055, 983055, 983055, 983055, 203010134,
    ),
    (
        7813216, -1337968528, -2073976608, 7446768, 73707552, -1598029710,
        74711105, 4370480, 69312672, 71610368, 947402856, 552087624,
        73998584, -1599066072, 69513232, -1602224079, 675479602, -1601175551,
        132148, -1336924125, 67371025, 75038738, 808984776, 674439336,
        805831700, 806887608, 5349584, 5376003, 545786953, 546835497,
        135475288, 205063252, 676531209, 1617305816, 986137, 983055,
        983055, 983055, 983055, 983055, 983055, 207183990,
    ),
    (
        7813216, -1337968528, -2141083424, -1340036880, 7438434, 7512256,
        946380960, -1607452552, 71369844, 608411648, 69279939, 606314672,
        810033315, 686333968, 3221752, 3317888, 106640, 132148,
        1155152, 8586243, -1596981230, 807938099, 68427976, 547882105,
        407445560, 405348360, 538452152, 135464017, 72622216, 403251352,
        205070424, 676536536, 202990821, 1007734, 983055, 983055,
        983055, 983055, 983055, 983055, 1617297423, 73993305,
    ),
)


def norm_rows(hidden_rows, norm_gain):
    values = hidden_rows.astype(jnp.float32)
    inverse_rms = lax.rsqrt(jnp.mean(values * values, axis=-1, keepdims=True) + 1e-06)
    return (values * inverse_rms * norm_gain).astype(jnp.bfloat16)


def expert_rows(row_block, weights):
    gate_part = jnp.dot(row_block, weights[0], preferred_element_type=jnp.float32)
    up_part = jnp.dot(row_block, weights[1], preferred_element_type=jnp.float32)
    hidden = (jax.nn.silu(gate_part) * up_part).astype(jnp.bfloat16)
    return lax.dot_general(
        hidden, weights[2], (((1,), (1,)), ((), ())), preferred_element_type=jnp.float32
    )


def gather_scatter_form(tokens, norm_gain, expert_ids, gate_probs, expert_weights):
    axes = ("ep", "dp")
    experts = lax.axis_size("ep") * lax.axis_size("dp")
    me = lax.axis_index(axes)
    steps_total, tok_count, width = tokens.shape
    rows = steps_total * tok_count
    normed = norm_rows(tokens.reshape(rows, width), norm_gain)
    share = gate_probs / jnp.sum(gate_probs, axis=-1, keepdims=True)
    hits = expert_ids[..., None] == lax.broadcasted_iota(jnp.int32, (1, 1, 1, experts), 3)
    dense_share = jnp.sum(jnp.where(hits, share[..., None], 0.0), axis=2).reshape(rows, experts)
    all_rows = lax.all_gather(normed, axes, tiled=True)
    all_share = lax.all_gather(dense_share, axes, tiled=True)
    mine = lax.broadcasted_iota(jnp.int32, (1, experts), 1) == me
    row_share = jnp.sum(jnp.where(mine, all_share, 0.0), axis=1, keepdims=True)
    expert_out = expert_rows(all_rows, expert_weights[0])
    weighted = (row_share * expert_out).astype(jnp.bfloat16)
    combined = lax.psum_scatter(weighted, axes, scatter_dimension=0, tiled=True)
    return combined.reshape(steps_total, tok_count, width)


def moe_kernel(
    tok_hbm, gain_hbm, ids_hbm, prob_hbm, w_hbm, out_ref,
    tok, gain, ids, prob, x, wv, hid, scale, ob, sr, ys, yr, zs, zr,
    in_sem, w_sem, x_recv, x_send, c_recv, c_send, y_recv, y_send, z_recv, z_send,
):
    steps, toks, width = tok.shape
    group = 4 * toks
    top = ids.shape[1]
    ff = wv.shape[2]
    cols = width // PIECES
    experts = lax.axis_size("ep") * lax.axis_size("dp")
    ep = lax.axis_index("ep")
    c = lax.axis_index("dp")
    z = ep // NY
    y = ep % NY
    me = ep * 2 + c

    sib = {"ep": ep, "dp": 1 - c}
    ynb = {"ep": z * NY + 1 - y, "dp": c}
    zup = {"ep": (z + 1) % NZ * NY + y, "dp": c}
    zdn = {"ep": (z + NZ - 1) % NZ * NY + y, "dp": c}
    zfar = {"ep": (NZ - 1 - z) * NY + y, "dp": c}
    can_up = z < NZ - 1
    can_dn = z > 0
    outer = (z == 0) | (z == NZ - 1)

    barrier = pltpu.get_barrier_semaphore()
    for peer in (sib, ynb):
        pl.semaphore_signal(barrier, inc=1, device_id=peer)

    @pl.when(can_up)
    def _():
        pl.semaphore_signal(barrier, inc=1, device_id=zup)

    @pl.when(can_dn)
    def _():
        pl.semaphore_signal(barrier, inc=1, device_id=zdn)

    if LEAPS:
        @pl.when(outer)
        def _():
            pl.semaphore_signal(barrier, inc=1, device_id=zfar)

    loads = [
        pltpu.make_async_copy(tok_hbm, tok, in_sem.at[0]),
        pltpu.make_async_copy(gain_hbm, gain, in_sem.at[1]),
        pltpu.make_async_copy(ids_hbm, ids, in_sem.at[2]),
        pltpu.make_async_copy(prob_hbm, prob, in_sem.at[3]),
    ]
    for load in loads:
        load.start()
    for i in range(3):
        pltpu.make_async_copy(w_hbm.at[0, i], wv.at[i], w_sem.at[i]).start()

    def choose(values, index):
        value = jnp.int32(values[0])
        for place in range(1, len(values)):
            value = jnp.where(index == place, jnp.int32(values[place]), value)
        return value

    words = [choose(column, 2 * z + c) for column in zip(*PLANS)]

    for load in loads:
        load.wait()

    def norm(s):
        x[s, z, c, y, :, :width] = norm_rows(tok[s], gain[...])

    def shares(s):
        probs = prob[s]
        share = probs / jnp.sum(probs, axis=0, keepdims=True)
        named = ids[s]
        row = lax.broadcasted_iota(jnp.int32, (2 * experts, toks), 0)
        both = jnp.zeros((2 * experts, toks), jnp.float32)
        for i in range(top):
            hit = (row == named[i : i + 1]) | (row == named[i : i + 1] + experts)
            both = jnp.where(hit, share[i : i + 1], both)
        high = both.astype(jnp.bfloat16).astype(jnp.float32)
        pieces = jnp.where(row < experts, high, both - high).astype(jnp.bfloat16)
        eye = (
            lax.broadcasted_iota(jnp.int32, (2 * experts, LANES), 0) + 2 * experts * s
            == lax.broadcasted_iota(jnp.int32, (2 * experts, LANES), 1)
        ).astype(jnp.float32).astype(jnp.bfloat16)
        return lax.dot_general(
            pieces, eye, (((0,), (0,)), ((), ())), preferred_element_type=jnp.float32
        )

    norm(0)
    x[0, z, c, y, :, width:] = (shares(0) + shares(1)).astype(jnp.bfloat16)
    peers = 2 + jnp.where(can_up, 1, 0) + jnp.where(can_dn, 1, 0)
    if LEAPS:
        peers = peers + jnp.where(outer, 1, 0)
    pl.semaphore_wait(barrier, peers)

    def x_copy(s, k, col, row, far, act, do):
        peer = (zup, zdn, ynb, sib, zfar)[act]
        for block, here in (
            (x.at[s, k, col, row], s == 0),
            (x.at[s, k, col, row, :, :width], s > 0),
        ):
            @pl.when(here)
            def _(block=block):
                do(pltpu.make_async_remote_copy(
                    block, block, x_send.at[s, k, far, act], x_recv.at[s, k, col, row],
                    device_id=peer,
                ))

    def c_copy(n, p):
        return pltpu.make_async_remote_copy(
            ob.at[n, p, 1 - c], sr.at[n, p], c_send.at[n, p], c_recv.at[n, p], device_id=sib
        )

    def y_copy(n, p):
        return pltpu.make_async_remote_copy(
            ys.at[n, p], yr.at[n, p], y_send.at[n, p], y_recv.at[n, p], device_id=ynb
        )

    def z_copy(n, p, far, source, target):
        return pltpu.make_async_remote_copy(
            zs.at[n, p, far], zr.at[source, n, p, far], z_send.at[n, p, far],
            z_recv.at[source, n, p, far], device_id={"ep": target * NY + y, "dp": c},
        )

    def start(copy):
        copy.start()

    def sent(copy):
        copy.wait_send()

    def got(copy):
        copy.wait_recv()

    def f32(value):
        return value.astype(jnp.float32)

    def do_relay(s, k, far, p, bits):
        row = jnp.where(far == 1, 1 - y, y)

        @pl.when(bits >= 32)
        def _():
            x_copy(s, k, c, row, far, 2, got)

        for act in range(4 + LEAPS):
            @pl.when(bits // 2**act % 2 == 1)
            def _(act=act):
                x_copy(s, k, c, row, far, act, start)

    def do_sent(s, k, far, p, bits):
        row = jnp.where(far == 1, 1 - y, y)
        for act in range(4 + LEAPS):
            @pl.when(bits // 2**act % 2 == 1)
            def _(act=act):
                x_copy(s, k, c, row, far, act, sent)

    def do_norm(s, k, far, p, bits):
        norm(1)

    def do_hidden(s, k, far, p, bits):
        @pl.when(bits >= 32)
        def _():
            for i in range(2):
                pltpu.make_async_copy(w_hbm.at[0, i], wv.at[i], w_sem.at[i]).wait()

        @pl.when(p == 0)
        def _():
            for row in range(NY):
                x_copy(s, k, 1 - c, row, 0, 3, got)

        @pl.when(far == 0)
        def _():
            @pl.when(p == 0)
            def _():
                scale[:group] = scales(s, k)

            hidden_part(x[s, k, :, :, :, :width].reshape(group, width), p, group)

        if PAIRS:
            @pl.when(far == 1)
            def _():
                @pl.when(p == 0)
                def _():
                    for row in range(NY):
                        x_copy(1, k, 1 - c, row, 0, 3, got)

                    for q in range(2):
                        scale[q * group : (q + 1) * group] = scales(q, k)

                hidden_part(x[:, k, :, :, :, :width].reshape(2 * group, width), p, 2 * group)

        @pl.when(bits % 2 == 1)
        def _():
            do_out(s, k, far, p, bits)

    def scales(s, k):
        lane = lax.broadcasted_iota(jnp.int32, (group, LANES), 1) - 2 * experts * s
        parts = f32(x[0, k, :, :, :, width:].reshape(group, LANES))
        mine = (lane == me) | (lane == me + experts)
        share = jnp.sum(jnp.where(mine, parts, 0.0), axis=1, keepdims=True)
        return jnp.broadcast_to(share, (group, LANES))

    def hidden_part(block, p, rows):
        for f in range(0, F_TILE, 256):
            here = pl.ds(pl.multiple_of(p * F_TILE + f, 256), 256)
            gate = jnp.dot(block, wv[0, :, here], preferred_element_type=jnp.float32)
            up = jnp.dot(block, wv[1, :, here], preferred_element_type=jnp.float32)
            hid[:rows, here] = (gate / (1.0 + jnp.exp(-gate)) * up).astype(jnp.bfloat16)

    def do_out(s, k, far, p, bits):
        @pl.when(bits >= 32)
        def _():
            pltpu.make_async_copy(w_hbm.at[0, 2], wv.at[2], w_sem.at[2]).wait()

        def out_part(rows):
            hidden = hid[:rows]
            tile = 256
            share = jnp.concatenate([scale[:rows]] * (tile // LANES), axis=1)
            for d in range(0, cols, tile):
                part = lax.dot_general(
                    hidden, wv[2, pl.ds(pl.multiple_of(p * cols + d, tile), tile), :],
                    (((1,), (1,)), ((), ())), preferred_element_type=jnp.float32,
                )
                done = (share * part).astype(jnp.bfloat16)
                for q in range(rows // group):
                    ob[(s + q) * NZ + k, p, :, :, :, d : d + tile] = (
                        done[q * group : (q + 1) * group].reshape(2, NY, toks, tile)
                    )
            for q in range(rows // group):
                c_copy((s + q) * NZ + k, p).start()

        @pl.when(far == 0)
        def _():
            out_part(group)

        if PAIRS:
            @pl.when(far == 1)
            def _():
                out_part(2 * group)

    def pair(n, p, row):
        return f32(ob[n, p, c, row]) + f32(sr[n, p, row])

    def first_waits(n, p, bits):
        @pl.when(bits % 2 == 1)
        def _():
            c_copy(n, p).wait_recv()

        @pl.when(bits // 2 % 2 == 1)
        def _():
            y_copy(n, p).wait_recv()

    def do_cross(s, k, far, p, bits):
        n = s * NZ + k
        first_waits(n, p, bits)
        ys[n, p] = pair(n, p, 1 - y).astype(jnp.bfloat16)
        y_copy(n, p).start()

    def do_pass(s, k, far, p, bits):
        n = s * NZ + k
        row = jnp.where(far == 1, 1 - y, y)
        first_waits(n, p, bits)

        step = jnp.where(k > z, 1, -1)
        before = jnp.clip(z - step, 0, NZ - 1)

        @pl.when(bits // 4 % 2 == 1)
        def _():
            z_copy(n, p, far, before, z).wait_recv()

        @pl.when(bits // 2 % 4 == 3)
        def _():
            zs[n, p, far] = (
                pair(n, p, row) + f32(yr[n, p]) + f32(zr[before, n, p, far])
            ).astype(jnp.bfloat16)

        @pl.when(bits // 2 % 4 == 2)
        def _():
            zs[n, p, far] = (pair(n, p, row) + f32(zr[before, n, p, far])).astype(jnp.bfloat16)

        @pl.when(bits // 2 % 4 == 1)
        def _():
            zs[n, p, far] = (pair(n, p, row) + f32(yr[n, p])).astype(jnp.bfloat16)

        @pl.when(bits // 2 % 4 == 0)
        def _():
            zs[n, p, far] = pair(n, p, row).astype(jnp.bfloat16)

        @pl.when(bits // 8 % 2 == 0)
        def _():
            z_copy(n, p, far, z, z + step).start()

        if DIRECT:
            @pl.when(bits // 8 % 2 == 1)
            def _():
                z_copy(n, p, far, z, k).start()

    def arrived(n, p, far, row, bits):
        total = pair(n, p, row)
        for source in range(NZ):
            named = bits // (4 * 2**source) % 2 == 1

            @pl.when(named)
            def _(source=source):
                z_copy(n, p, far, source, (z + 1) % NZ).wait_recv()

            total = total + jnp.where(named, f32(zr[source, n, p, far]), 0.0)
        return total

    def do_hand(s, k, far, p, bits):
        n = s * NZ + k
        first_waits(n, p, bits % 2)
        ys[n, p] = arrived(n, p, 1, 1 - y, bits).astype(jnp.bfloat16)
        y_copy(n, p).start()

    def do_final(s, k, far, p, bits):
        n = s * NZ + k
        first_waits(n, p, bits % 2 + 2)
        total = arrived(n, p, 0, y, bits) + f32(yr[n, p])
        here = pl.ds(pl.multiple_of(p * cols, cols), cols)
        out_ref[s, :, here] = total.astype(jnp.bfloat16)

    def do_settle(s, k, far, p, bits):
        n = s * NZ + k
        c_copy(n, p).wait_send()

        @pl.when(bits % 2 == 1)
        def _():
            y_copy(n, p).wait_send()

        for lane in range(2):
            @pl.when(bits // (2 + 2 * lane) % 2 == 1)
            def _(lane=lane):
                z_copy(n, p, lane, z, (z + 1) % NZ).wait_send()

    kinds = (
        (do_relay, do_hidden, do_out),
        (do_pass, do_cross, do_hand, do_final),
        (do_norm, do_sent, do_settle),
    )

    def obey(code):
        kind = code % 16
        s = code // 16 % 2
        k = code // 32 % 4
        far = code // 128 % 2
        p = code // 256 % 4
        bits = code // 1024
        first = 0
        for some in kinds:
            @pl.when((kind >= first) & (kind < first + len(some)))
            def _(first=first, some=some):
                for number, body in enumerate(some):
                    @pl.when(kind == first + number)
                    def _(body=body):
                        body(s, k, far, p, bits)

            first += len(some)

    blocks = len(words) // ROW

    def block(b, carry):
        row = [choose(words[j::ROW], b) for j in range(ROW)]

        def entry(i, carry):
            word = choose(row, i // 2)
            obey(jnp.where(i % 2 == 0, word & 65535, (word >> 16) & 65535))
            return carry

        lax.fori_loop(0, 2 * ROW, entry, 0)
        return carry

    lax.fori_loop(0, blocks, block, 0)


def kernel_form(tokens, norm_gain, expert_ids, gate_probs, expert_weights):
    steps, toks, width = tokens.shape
    top = expert_ids.shape[2]
    ff = expert_weights.shape[3]
    groups = steps * NZ
    cols = width // PIECES
    half = jnp.bfloat16
    hbm = pl.BlockSpec(memory_space=pltpu.MemorySpace.HBM)
    dma = pltpu.SemaphoreType.DMA
    rows = groups * 4 * toks
    return pl.pallas_call(
        moe_kernel,
        out_shape=jax.ShapeDtypeStruct((steps, toks, width), half),
        in_specs=[hbm, hbm, hbm, hbm, hbm],
        out_specs=pl.BlockSpec(memory_space=pltpu.VMEM),
        scratch_shapes=[
            pltpu.VMEM((steps, toks, width), half),
            pltpu.VMEM((1, width), jnp.float32),
            pltpu.VMEM((steps, top, toks), jnp.int32),
            pltpu.VMEM((steps, top, toks), jnp.float32),
            pltpu.VMEM((steps, NZ, 2, NY, toks, width + LANES), half),
            pltpu.VMEM((3, width, ff), half),
            pltpu.VMEM((8 * toks, ff), half),
            pltpu.VMEM((8 * toks, LANES), jnp.float32),
            pltpu.VMEM((groups, PIECES, 2, NY, toks, cols), half),
            pltpu.VMEM((groups, PIECES, NY, toks, cols), half),
            pltpu.VMEM((groups, PIECES, toks, cols), half),
            pltpu.VMEM((groups, PIECES, toks, cols), half),
            pltpu.VMEM((groups, PIECES, NY, toks, cols), half),
            pltpu.VMEM((NZ, groups, PIECES, NY, toks, cols), half),
            dma((4,)),
            dma((3,)),
            dma((steps, NZ, 2, NY)),
            dma((steps, NZ, 2, 5)),
            dma((groups, PIECES)),
            dma((groups, PIECES)),
            dma((groups, PIECES)),
            dma((groups, PIECES)),
            dma((NZ, groups, PIECES, NY)),
            dma((groups, PIECES, NY)),
        ],
        compiler_params=pltpu.CompilerParams(
            collective_id=0, has_side_effects=True, vmem_limit_bytes=64 * 1024 * 1024
        ),
        cost_estimate=pl.CostEstimate(
            flops=6 * rows * width * ff, bytes_accessed=6 * width * ff, transcendentals=rows * ff
        ),
    )(
        tokens,
        norm_gain.reshape(1, width),
        expert_ids.transpose(0, 2, 1),
        gate_probs.transpose(0, 2, 1),
        expert_weights,
    )


def solution(mesh):
    in_specs = (
        P(None, ("grp", "ep", "dp"), None),
        P(),
        P(None, ("grp", "ep", "dp"), None),
        P(None, ("grp", "ep", "dp"), None),
        P(("ep", "dp"), None, None, None),
    )
    out_specs = P(None, ("grp", "ep", "dp"), None)
    small = mesh.shape["ep"] == NZ * NY and mesh.shape["dp"] == 2
    shards = kernel_form if small else gather_scatter_form
    return jax.shard_map(shards, mesh=mesh, in_specs=in_specs, out_specs=out_specs, check_vma=False)
```
